32 devices in a mesh: groups: 2 (over y), ctx: 4 (over z), head: 2 (over x), sub: 2 (over core).
Axes of the slice: x: 2, y: 2, z: 4, core: 2. Of those that a mesh axis runs over, the one named last changes fastest.
Arguments:
- queries: bfloat16 [2048, 64, 128], P(('groups', 'ctx', 'sub'), 'head'), parts along dimension 0, may hold values from -6 to 6
- keys: bfloat16 [2048, 4, 128], P(('groups', 'ctx', 'sub'), 'head'), parts along dimension 0, may hold values from -6 to 6
- values: bfloat16 [2048, 4, 128], P(('groups', 'ctx', 'sub'), 'head'), parts along dimension 0, may hold values from -6 to 6
- grad_out: bfloat16 [2048, 64, 128], P(('groups', 'ctx', 'sub'), 'head'), parts along dimension 0, may hold values from -9 to 9
- row_lse: float32 [2048, 64], P(('groups', 'ctx', 'sub'), 'head'), parts along dimension 0, may hold values from 5.5 to 6.5
- row_delta: float32 [2048, 64], P(('groups', 'ctx', 'sub'), 'head'), parts along dimension 0, may hold values from -24 to 24
- doc_ids: int32 [2048], P(('groups', 'ctx', 'sub')), parts along dimension 0, may hold values from 0 to 3, never falling along the last dimension, each value on 1 to 512 neighbouring positions
- pairs: int32 [16, 2], P('groups'), parts along dimension 0, may hold values from 0 to 7, as said below
Outputs:
- grad_queries: float32 [2048, 64, 128], P(('groups', 'ctx', 'sub'), 'head'), parts along dimension 0
- grad_keys: float32 [2048, 4, 128], P(('groups', 'ctx', 'sub'), 'head'), parts along dimension 0
- grad_values: float32 [2048, 4, 128], P(('groups', 'ctx', 'sub'), 'head'), parts along dimension 0
The draws below stay inside these ranges and needn't reach their ends.
There are 2 independent parts, one for each index of `groups`. The reference program is written for one: setup_inputs(seed, part) draws one part's arguments, and reference() takes and returns one part's arrays. A program takes and returns all parts, laid end to end along the dimension named above; each array names one. Nothing has to cross between parts.
Inputs may be any that keep to these rules, and one draw needn't show every extreme that they name: `pairs`: row c holds two different span indices, neither equal to c. `doc_ids`: never falls along the tokens; every document appears.
All inputs are finite; a program needn't handle non-finite values.
Results may differ from the reference program's by a relative error of at most 0.0046.
Values may be sent and summed in bfloat16 or wider, within the bound.
A program may use at most 64 MiB of HBM per device.

```python
import math
import jax
import jax.numpy as jnp
import numpy as np
from jax import lax

QH = 64
KVH = 4
HD = 128
TOK_DEV = 128
DOCS = 4
NCHUNK = 8
TOKENS = 1024


def draw_pairs(key, part):
    key_first, key_second = jax.random.split(jax.random.fold_in(key, 11))
    first = jax.random.randint(key_first, (NCHUNK,), 0, NCHUNK - 1)
    first = first.at[0].set(NCHUNK - 2).at[NCHUNK - 1].set(0)
    second = jax.random.randint(key_second, (NCHUNK,), 0, NCHUNK - 2)
    span_rows = jnp.arange(NCHUNK, dtype=jnp.int32)
    listed_one = (span_rows + 1 + first) % NCHUNK
    listed_two = (span_rows + 1 + (first + 1 + second) % (NCHUNK - 1)) % NCHUNK
    return jnp.stack([listed_one, listed_two], axis=1).astype(jnp.int32)


def level_of(own_key, extent, pieces, low, top_value):
    gain, own = 1.0, jax.random.fold_in(own_key, 6)
    for position, parts in pieces:
        heights = jnp.exp(jax.random.uniform(jax.random.fold_in(own, position), (parts,), jnp.float32, low / len(pieces), top_value / len(pieces)))
        gain = gain * jnp.repeat(heights, extent[position] // parts).reshape([-1 if axis == position else 1 for axis in range(len(extent))])
    return gain


def profile(number_of, total, most, lean):
    weights = [(1 << 20) // math.isqrt(standing ** lean) + 1 for standing in range(2, number_of + 1)]
    spare, given = total - most - (number_of - 1), [1] * (number_of - 1)
    while spare > 0:
        free = [i for i in range(number_of - 1) if given[i] < most]
        pool, remaining = sum([weights[i] for i in free]), spare
        for i in free:
            addition = min(most - given[i], max(1, remaining * weights[i] // pool), spare)
            given[i] = given[i] + addition
            spare = spare - addition
    return np.array([most] + given)


def ragged(rng, count, total, most, slope):
    if count == 2:
        one = jax.random.randint(rng, (), max(1, total - most), min(most, total - 1) + 1)
        return jnp.stack([one, total - one])
    lengths = jnp.asarray(profile(count, total, most, slope), jnp.int32)
    pairs = (count - 1) // 2
    donor, taker = lengths[1:1 + 2 * pairs:2], lengths[2:2 + 2 * pairs:2]
    slack = jnp.minimum(donor - 1, most - taker)
    passed = jax.random.randint(jax.random.fold_in(rng, 1), (pairs,), 0, 1 << 20) % (slack + 1)
    lengths = lengths.at[1:1 + 2 * pairs:2].set(donor - passed).at[2:2 + 2 * pairs:2].set(taker + passed)
    return lengths[jax.random.permutation(jax.random.fold_in(rng, 2), count)]


def noise(key, dims, deviation, most, pieces=(), kind=jnp.bfloat16):
    array = jax.random.normal(key, dims, jnp.float32) * deviation
    if len(pieces) > 0:
        array = level_of(key, dims, pieces, -0.22, 0.18) * array
    return jnp.clip(array, min=-most, max=most).astype(kind)


def setup_inputs(seed: int = 0, part: int = 0) -> dict:
    key_of = jax.random.split(jax.random.key(seed), 9)
    part_splits = jax.random.split(jax.random.fold_in(key_of[8], part), 9)
    return {
        "queries": noise(part_splits[0], (TOKENS, QH, HD), 1.0, 6.0, ((0, 8), (1, 2))),
        "keys": noise(part_splits[1], (TOKENS, KVH, HD), 1.0, 6.0, ((0, 8), (1, 2))),
        "values": noise(part_splits[2], (TOKENS, KVH, HD), 1.0, 6.0, ((0, 8), (1, 2))),
        "grad_out": noise(part_splits[3], (TOKENS, QH, HD), 1.5, 9.0, ((0, 8), (1, 2))),
        "row_lse": jnp.clip(5.5 + 1.0 * jax.random.uniform(part_splits[4], (TOKENS, QH), jnp.float32) ** level_of(part_splits[4], (TOKENS, QH), ((0, 8), (1, 2)), -0.2, 0.2), 5.5, 6.5),
        "row_delta": noise(part_splits[5], (TOKENS, QH), 4.0, 24.0, ((0, 8), (1, 2)), jnp.float32),
        "doc_ids": jnp.searchsorted(jnp.cumsum(ragged(part_splits[6], DOCS, TOKENS, TOKENS // 2, 0)), jnp.arange(TOKENS), side="right").astype(jnp.int32),
        "pairs": draw_pairs(jax.random.fold_in(jax.random.fold_in(key_of[8], part), 71), part),
    }


def block_terms(query_blk, upstream, log_norm, row_terms, key_blk, value_blk, allowed, factor):
    query_wide = query_blk.astype(jnp.float32)
    upstream_wide = upstream.astype(jnp.float32)
    key_wide = key_blk.astype(jnp.float32)
    value_wide = value_blk.astype(jnp.float32)
    scores = jnp.einsum('tghd,kgd->tghk', query_wide, key_wide) * factor
    probs = jnp.exp(scores - log_norm[..., None])
    if allowed is not None:
        probs = jnp.where(allowed[:, None, None, :], probs, 0.0)
    grad_probs = jnp.einsum('tghd,kgd->tghk', upstream_wide, value_wide)
    grad_scores = probs * (grad_probs - row_terms[..., None])
    probs_low = lax.optimization_barrier(probs.astype(jnp.bfloat16)).astype(jnp.float32)
    scores_low = lax.optimization_barrier(grad_scores.astype(jnp.bfloat16)).astype(jnp.float32)
    grad_val = jnp.einsum('tghk,tghd->kgd', probs_low, upstream_wide)
    grad_key = jnp.einsum('tghk,tghd->kgd', scores_low, query_wide) * factor
    grad_query = jnp.einsum('tghk,kgd->tghd', scores_low, key_wide) * factor
    return grad_query, grad_key, grad_val


def reference(queries, keys, values, grad_out, row_lse, row_delta, doc_ids, pairs):
    grouped = QH // KVH
    factor = HD ** -0.5
    query_all = queries.reshape(NCHUNK, TOK_DEV, KVH, grouped, HD)
    upstream_all = grad_out.reshape(NCHUNK, TOK_DEV, KVH, grouped, HD)
    keys_all = keys.reshape(NCHUNK, TOK_DEV, KVH, HD)
    values_all = values.reshape(NCHUNK, TOK_DEV, KVH, HD)
    norm_all = row_lse.reshape(NCHUNK, TOK_DEV, KVH, grouped)
    terms_all = row_delta.reshape(NCHUNK, TOK_DEV, KVH, grouped)
    docs_all = doc_ids.reshape(NCHUNK, TOK_DEV)
    positions = jnp.arange(TOK_DEV, dtype=jnp.int32)
    causal = positions[:, None] >= positions[None, :]

    def advance(totals, span_idx):
        key_total, value_total = totals
        query_blk = query_all[span_idx]
        upstream = upstream_all[span_idx]
        log_norm = norm_all[span_idx]
        row_terms = terms_all[span_idx]
        docs = docs_all[span_idx]
        allowed = causal & (docs[:, None] == docs[None, :])
        query_sum, key_part, value_part = block_terms(query_blk, upstream, log_norm, row_terms, keys_all[span_idx], values_all[span_idx], allowed, factor)
        key_total = key_total.at[span_idx].add(key_part)
        value_total = value_total.at[span_idx].add(value_part)
        for which in range(2):
            target = pairs[span_idx, which]
            query_part, key_part, value_part = block_terms(query_blk, upstream, log_norm, row_terms, keys_all[target], values_all[target], None, factor)
            query_sum = query_sum + query_part
            key_total = key_total.at[target].add(key_part)
            value_total = value_total.at[target].add(value_part)
        return (key_total, value_total), query_sum

    zero_grads = jnp.zeros((NCHUNK, TOK_DEV, KVH, HD), jnp.float32)
    (key_total, value_total), query_grads = lax.scan(advance, (zero_grads, zero_grads), jnp.arange(NCHUNK, dtype=jnp.int32))
    return (query_grads.reshape(TOKENS, QH, HD), key_total.reshape(TOKENS, KVH, HD), value_total.reshape(TOKENS, KVH, HD))
```

```python
import functools
import math

import jax
import jax.numpy as jnp
from jax import lax
from jax.experimental import pallas as pl
from jax.experimental.pallas import tpu as pltpu
from jax.sharding import PartitionSpec as P

BF = jnp.bfloat16
F32 = jnp.float32
MESH = pl.DeviceIdType.MESH


def pieces_of(x):
    hi = x.astype(BF)
    rest = x - hi.astype(F32)
    mid = rest.astype(BF)
    lo = (rest - mid.astype(F32)).astype(BF)
    return hi, mid, lo


def kernel(
    dims,
    pairs_ref, docs_ref, lse_ref, delta_ref, keys_ref, vals_ref, q_hbm, up_hbm,
    dq_vm, dk_ref, dv_ref,
    own_ref, q_vm, up_vm, qa, da, bias, kfar, vfar, kloc, vloc,
    dk_loc, dv_loc, kv_all, send_a, recv_a, send_b, recv_b,
    in_sem, z_send, p_send, z_recv, p_recv, a_send, a_recv, b_send, b_recv,
):
    zs, ss, rows, kvh, grp, hd, tile_tok = dims
    spans = zs * ss
    stripe = rows // spans
    factor = hd ** -0.5
    scale2 = factor * math.log2(math.e)
    z = lax.axis_index("ctx")
    s = lax.axis_index("sub")
    me = z * ss + s
    tiles = rows // tile_tok
    tr = tile_tok * grp

    ins = [
        pltpu.make_async_copy(q_hbm, q_vm, in_sem.at[0]),
        pltpu.make_async_copy(up_hbm, up_vm, in_sem.at[1]),
    ]
    for c in ins:
        c.start()

    barrier = pltpu.get_barrier_semaphore()

    def peer_of(off):
        d = lax.rem(me + off, spans)
        return d, d // ss, lax.rem(d, ss)

    def greet(dz, ds):
        pl.semaphore_signal(barrier, inc=1, device_id={"ctx": dz, "sub": ds}, device_id_type=MESH)

    greet(z, 1 - s)

    @pl.when(z > 0)
    def _():
        greet(z - 1, s)

    @pl.when(z < zs - 1)
    def _():
        greet(z + 1, s)


    pick_t = lax.broadcasted_iota(jnp.int32, (rows, rows * kvh), 0)
    pick_r = lax.broadcasted_iota(jnp.int32, (rows, rows * kvh), 1)
    for g in range(kvh):
        pick = jnp.where(pick_r == pick_t * kvh + g, 1.0, 0.0).astype(BF)
        for part, ref in enumerate((keys_ref, vals_ref)):
            took = jnp.dot(pick, ref[...], preferred_element_type=F32)
            own_ref[g, :, part * hd:(part + 1) * hd] = took.astype(BF)

    pos_t = lax.broadcasted_iota(jnp.int32, (rows, rows), 0)
    pos_u = lax.broadcasted_iota(jnp.int32, (rows, rows), 1)
    doc_u = jnp.broadcast_to(docs_ref[...].astype(F32), (rows, rows))
    doc_t = doc_u.T
    bias[...] = jnp.where((pos_t >= pos_u) & (doc_u == doc_t), 0.0, -3e38)

    heads = kvh * grp
    put_h = lax.broadcasted_iota(jnp.int32, (heads, hd), 0)
    put_l = lax.broadcasted_iota(jnp.int32, (heads, hd), 1)

    def lanes_of(x):
        total = jnp.zeros((rows, hd), F32)
        for i, piece in enumerate(pieces_of(x)):
            place = jnp.where(put_l == put_h + i * heads, 1.0, 0.0).astype(BF)
            total = total + lax.dot_general(
                piece, place, (((0,), (0,)), ((), ())), preferred_element_type=F32
            )
        return total.astype(BF)

    lse_l = lanes_of(lse_ref[...] * (hd ** 0.5))
    del_l = lanes_of(delta_ref[...])
    row_h = lax.broadcasted_iota(jnp.int32, (grp, hd), 0)
    row_l = lax.broadcasted_iota(jnp.int32, (grp, hd), 1)
    used = lax.broadcasted_iota(jnp.int32, (rows, hd), 1) < 3 * heads
    neg = jnp.where(used, -1.0, 0.0).astype(BF)

    ends = jnp.where(z > 0, 1, 0) + jnp.where(z < zs - 1, 1, 0)
    pl.semaphore_wait(barrier, 1 + ends)


    other = 1 - s

    def to_line(g, slot, src, dz, way):
        return pltpu.make_async_remote_copy(
            src_ref=src, dst_ref=kv_all[g].at[slot],
            send_sem=z_send.at[g, slot, way], recv_sem=z_recv.at[g, slot],
            device_id={"ctx": dz, "sub": s}, device_id_type=MESH)

    def to_partner(g, slot, src):
        return pltpu.make_async_remote_copy(
            src_ref=src, dst_ref=kv_all[g].at[slot],
            send_sem=p_send.at[g, slot], recv_sem=p_recv.at[g, slot],
            device_id={"ctx": z, "sub": other}, device_id_type=MESH)

    def spread(g, slot, src, do, right, left):
        @pl.when(right)
        def _():
            c = to_line(g, slot, src, z + 1, 0)
            c.start() if do else c.wait_send()

        @pl.when(left)
        def _():
            c = to_line(g, slot, src, z - 1, 1)
            c.start() if do else c.wait_send()

        c = to_partner(g, slot, src)
        c.start() if do else c.wait_send()

    def own_step(g, do):
        spread(g, me, own_ref.at[g], do, z < zs - 1, z > 0)

    def relay_step(g, j, do):
        @pl.when(z - j >= 0)
        def _():
            slot = (z - j) * ss + s
            if do:
                to_line(g, slot, own_ref.at[g], z, 0).wait_recv()
            spread(g, slot, kv_all[g].at[slot], do, z < zs - 1, z < 0)

        @pl.when(z + j < zs)
        def _():
            slot = (z + j) * ss + s
            if do:
                to_line(g, slot, own_ref.at[g], z, 0).wait_recv()
            spread(g, slot, kv_all[g].at[slot], do, z < 0, z > 0)

    def partner_wait(g):
        for a in range(zs):
            slot = a * ss + other
            to_partner(g, slot, own_ref.at[g]).wait_recv()

    for g in range(kvh):
        own_step(g, True)

    for c in ins:
        c.wait()

    def attend(g, qa, da, kcat, vcat, local):
        nk = kcat.shape[0]

        def step(i, carry):
            dk, dv = carry
            rs = pl.ds(pl.multiple_of(i * tr, tr), tr)
            ts = pl.ds(pl.multiple_of(i * tile_tok, tile_tok), tile_tok)
            qt = qa[rs, :]
            ut = da[rs, :]
            nt = (((1,), (1,)), ((), ()))
            x = lax.dot_general(qt, kcat[...], nt, preferred_element_type=F32)
            y = lax.dot_general(ut, vcat[...], nt, preferred_element_type=F32)
            if local:
                x = (x.reshape(tile_tok, grp, nk) + bias[ts, :][:, None, :]).reshape(tr, nk)
            p = jnp.exp2(x * scale2)
            ds_low = (p * y).astype(BF)
            p_low = p.astype(BF)
            dq = jnp.dot(ds_low, kcat[:, :hd], preferred_element_type=F32)
            tn = (((0,), (0,)), ((), ()))
            dk = dk + lax.dot_general(ds_low, qt[:, :hd], tn, preferred_element_type=F32)
            dv = dv + lax.dot_general(p_low, ut[:, :hd], tn, preferred_element_type=F32)
            sl = pl.ds(g * grp, grp)
            dq = dq.reshape(tile_tok, grp, hd)
            if local:
                dq_vm[ts, sl, :] = dq
            else:
                dq_vm[ts, sl, :] = (dq_vm[ts, sl, :] + dq) * factor
            return dk, dv

        zero = jnp.zeros((nk, hd), F32)
        return lax.fori_loop(0, tiles, step, (zero, zero))

    def near(g):
        build_g(g)
        kloc[:, :hd] = own_ref[g, :, :hd]
        kloc[:, hd:] = neg
        vloc[:, :hd] = own_ref[g, :, hd:]
        vloc[:, hd:] = neg
        dk, dv = attend(g, qa.at[g], da.at[g], kloc, vloc, True)
        dk_loc[g] = dk
        dv_loc[g] = dv

    def build_g(g):
        head = row_h + g * grp
        hit = (row_l == head) | (row_l == head + heads) | (row_l == head + 2 * heads)
        keep = jnp.where(hit, 1.0, 0.0).astype(BF)
        sl = pl.ds(g * grp, grp)
        qa[g, :, :hd] = q_vm[:, sl, :].reshape(rows * grp, hd)
        da[g, :, :hd] = up_vm[:, sl, :].reshape(rows * grp, hd)
        qa[g, :, hd:] = (lse_l[:, None, :] * keep[None]).reshape(rows * grp, hd)
        da[g, :, hd:] = (del_l[:, None, :] * keep[None]).reshape(rows * grp, hd)

    def a_copy(g, off):
        d, dz, ds = peer_of(off)
        return pltpu.make_async_remote_copy(
            src_ref=send_a.at[g, d], dst_ref=recv_a.at[g, me],
            send_sem=a_send.at[g, off], recv_sem=a_recv.at[g, off],
            device_id={"ctx": dz, "sub": ds}, device_id_type=MESH)

    def b_copy(g, off):
        d, dz, ds = peer_of(off)
        return pltpu.make_async_remote_copy(
            src_ref=send_b.at[g, d], dst_ref=recv_b.at[g, me],
            send_sem=b_send.at[g, off], recv_sem=b_recv.at[g, off],
            device_id={"ctx": dz, "sub": ds}, device_id_type=MESH)

    def far(g):
        for j in range(2):
            blk = kv_all[g][pairs_ref[j, me]]
            js = pl.ds(j * rows, rows)
            kfar[js, :hd] = blk[:, :hd]
            kfar[js, hd:] = neg
            vfar[js, :hd] = blk[:, hd:]
            vfar[js, hd:] = neg
        dk, dv = attend(g, qa.at[g], da.at[g], kfar, vfar, False)
        for j in range(2):
            js = slice(j * rows, (j + 1) * rows)
            send_a[g, :, j, :, :hd] = dk[js].astype(BF).reshape(spans, stripe, hd)
            send_a[g, :, j, :, hd:] = dv[js].astype(BF).reshape(spans, stripe, hd)
        recv_a[g, me] = send_a[g, me]
        for off in range(1, spans):
            a_copy(g, off).start()

    def combine(g):
        for off in range(1, spans):
            a_copy(g, off).wait_recv()

        def owner(o, _):
            total = jnp.zeros((stripe, 2 * hd), F32)
            for src in range(spans):
                for j in range(2):
                    got = recv_a[g, src, j].astype(F32)
                    total = total + jnp.where(pairs_ref[j, src] == o, got, 0.0)
            send_b[g, o] = total.astype(BF)
            return 0

        lax.fori_loop(0, spans, owner, 0)
        recv_b[g, me] = send_b[g, me]
        for off in range(1, spans):
            b_copy(g, off).start()

    def finish(g):
        for off in range(1, spans):
            b_copy(g, off).wait_recv()
        home = recv_b[g].reshape(rows, 2 * hd).astype(F32)
        at = pl.ds(g, rows, stride=kvh)
        dk_ref[at, :] = (dk_loc[g] + home[:, :hd]) * factor
        dv_ref[at, :] = dv_loc[g] + home[:, hd:]

    for g in range(kvh):
        near(g)
        relay_step(g, 1, True)
        if g > 0 and zs > 2:
            relay_step(g - 1, 2, True)
    for g in range(kvh):
        first = 2 if g == kvh - 1 else 3
        for j in range(first, zs):
            relay_step(g, j, True)
    for g in range(kvh):
        own = own_ref[g]
        kv_all[g][me] = own
    for g in range(kvh):
        partner_wait(g)
        far(g)
    for g in range(kvh):
        combine(g)
    for g in range(kvh):
        finish(g)
    for g in range(kvh):
        own_step(g, False)
        for j in range(1, zs):
            relay_step(g, j, False)
        for off in range(1, spans):
            a_copy(g, off).wait_send()
            b_copy(g, off).wait_send()


def tail_kernel(dq_vm, dk_vm, dv_vm, dq_out, dk_out, dv_out, sems):
    copies = [
        pltpu.make_async_copy(src, dst, sems.at[i])
        for i, (src, dst) in enumerate(((dq_vm, dq_out), (dk_vm, dk_out), (dv_vm, dv_out)))
    ]
    for c in copies:
        c.start()
    for c in copies:
        c.wait()


def written(dq, dk, dv):
    return pl.pallas_call(
        tail_kernel,
        out_shape=tuple(jax.ShapeDtypeStruct(x.shape, F32) for x in (dq, dk, dv)),
        in_specs=[pl.BlockSpec(memory_space=pltpu.VMEM)] * 3,
        out_specs=(pl.BlockSpec(memory_space=pltpu.HBM),) * 3,
        scratch_shapes=[pltpu.SemaphoreType.DMA((3,))],
        compiler_params=pltpu.CompilerParams(vmem_limit_bytes=4 * 1024 * 1024),
        name="write_out",
    )(dq, dk, dv)


def fused(zs, ss, queries, keys, values, grad_out, row_lse, row_delta, doc_ids, pairs):
    rows, qh, hd = queries.shape
    kvh = keys.shape[1]
    grp = qh // kvh
    spans = zs * ss
    stripe = rows // spans
    tile_tok = 128
    vm = pl.BlockSpec(memory_space=pltpu.VMEM)
    sm = pl.BlockSpec(memory_space=pltpu.SMEM)
    hbm = pl.BlockSpec(memory_space=pltpu.HBM)
    dma = pltpu.SemaphoreType.DMA
    dq, dk, dv = pl.pallas_call(
        functools.partial(kernel, (zs, ss, rows, kvh, grp, hd, tile_tok)),
        out_shape=(
            pltpu.VMEM((rows, qh, hd), F32),
            pltpu.VMEM((rows * kvh, hd), F32),
            pltpu.VMEM((rows * kvh, hd), F32),
        ),
        in_specs=[sm, vm, vm, vm, vm, vm, hbm, hbm],
        out_specs=(vm, vm, vm),
        scratch_shapes=[
            pltpu.VMEM((kvh, rows, 2 * hd), BF),
            pltpu.VMEM((rows, qh, hd), BF),
            pltpu.VMEM((rows, qh, hd), BF),
            pltpu.VMEM((kvh, rows * grp, 2 * hd), BF),
            pltpu.VMEM((kvh, rows * grp, 2 * hd), BF),
            pltpu.VMEM((rows, rows), F32),
            pltpu.VMEM((2 * rows, 2 * hd), BF),
            pltpu.VMEM((2 * rows, 2 * hd), BF),
            pltpu.VMEM((rows, 2 * hd), BF),
            pltpu.VMEM((rows, 2 * hd), BF),
            pltpu.VMEM((kvh, rows, hd), F32),
            pltpu.VMEM((kvh, rows, hd), F32),
            [pltpu.VMEM((spans, rows, 2 * hd), BF) for _ in range(kvh)],
            pltpu.VMEM((kvh, spans, 2, stripe, 2 * hd), BF),
            pltpu.VMEM((kvh, spans, 2, stripe, 2 * hd), BF),
            pltpu.VMEM((kvh, spans, stripe, 2 * hd), BF),
            pltpu.VMEM((kvh, spans, stripe, 2 * hd), BF),
            dma((2,)),
            dma((kvh, spans, 2)),
            dma((kvh, spans)),
            dma((kvh, spans)),
            dma((kvh, spans)),
            dma((kvh, spans)),
            dma((kvh, spans)),
            dma((kvh, spans)),
            dma((kvh, spans)),
        ],
        compiler_params=pltpu.CompilerParams(collective_id=0, has_side_effects=True),
        name="span_grads",
    )(
        pairs.T, doc_ids.reshape(1, rows), row_lse.T, row_delta.T,
        keys.reshape(rows * kvh, hd), values.reshape(rows * kvh, hd), queries, grad_out,
    )
    dq, dk, dv = written(dq, dk, dv)
    return dq, dk.reshape(rows, kvh, hd), dv.reshape(rows, kvh, hd)


QH = 64
KVH = 4


def block_terms(query_blk, upstream, log_norm, row_terms, key_blk, value_blk, allowed, factor):
    scores = (
        jnp.einsum("tghd,kgd->tghk", query_blk, key_blk, preferred_element_type=jnp.float32)
        * factor
    )
    probs = jnp.exp(scores - log_norm[..., None])
    if allowed is not None:
        probs = jnp.where(allowed[:, None, None, :], probs, 0.0)
    grad_probs = jnp.einsum(
        "tghd,kgd->tghk", upstream, value_blk, preferred_element_type=jnp.float32
    )
    grad_scores = probs * (grad_probs - row_terms[..., None])
    probs_low = probs.astype(jnp.bfloat16)
    scores_low = grad_scores.astype(jnp.bfloat16)
    grad_val = jnp.einsum("tghk,tghd->kgd", probs_low, upstream, preferred_element_type=jnp.float32)
    grad_key = (
        jnp.einsum("tghk,tghd->kgd", scores_low, query_blk, preferred_element_type=jnp.float32)
        * factor
    )
    grad_query = (
        jnp.einsum("tghk,kgd->tghd", scores_low, key_blk, preferred_element_type=jnp.float32)
        * factor
    )
    return (grad_query, grad_key, grad_val)


def body(zs, ss, queries, keys, values, grad_out, row_lse, row_delta, doc_ids, pairs):
    grp = queries.shape[1] // keys.shape[1]
    if (
        ss == 2
        and queries.shape[0] % (16 * zs * ss) == 0
        and grp % 16 == 0
        and 3 * queries.shape[1] <= queries.shape[2]
    ):
        return fused(
            zs, ss, queries, keys, values, grad_out, row_lse, row_delta, doc_ids, pairs
        )
    rows_here = queries.shape[0]
    heads_here = keys.shape[1]
    head_dim = keys.shape[2]
    grouped = QH // KVH
    factor = head_dim ** (-0.5)
    spans = lax.axis_size(("ctx", "sub"))
    stripe = rows_here // spans
    query_blk = queries.reshape(rows_here, heads_here, grouped, head_dim)
    upstream = grad_out.reshape(rows_here, heads_here, grouped, head_dim)
    log_norm = row_lse.reshape(rows_here, heads_here, grouped)
    row_terms = row_delta.reshape(rows_here, heads_here, grouped)
    positions = jnp.arange(rows_here, dtype=jnp.int32)
    allowed = (positions[:, None] >= positions[None, :]) & (doc_ids[:, None] == doc_ids[None, :])
    query_sum, key_local, value_local = block_terms(
        query_blk, upstream, log_norm, row_terms, keys, values, allowed, factor
    )
    stacked = jnp.concatenate([keys, values], axis=2).reshape(rows_here, heads_here * 2 * head_dim)
    features = stacked.shape[1]
    spread = lax.all_to_all(
        stacked.reshape(spans, stripe, features),
        ("ctx", "sub"),
        split_axis=0,
        concat_axis=0,
        tiled=True,
    )
    wanted = jnp.take(spread, pairs.T, axis=0)
    remote = lax.all_to_all(
        wanted, ("ctx", "sub"), split_axis=1, concat_axis=1, tiled=True
    ).reshape(2, rows_here, features)
    remote = remote.reshape(2, rows_here, heads_here, 2 * head_dim)
    returned = []
    for which in range(2):
        far_keys = remote[which, :, :, :head_dim]
        far_values = remote[which, :, :, head_dim:]
        query_part, key_part, value_part = block_terms(
            query_blk, upstream, log_norm, row_terms, far_keys, far_values, None, factor
        )
        query_sum = query_sum + query_part
        returned.append(
            jnp.concatenate([key_part, value_part], axis=2).reshape(rows_here, features)
        )
    outgoing = jnp.stack(returned).reshape(2, spans, stripe, features)
    incoming = lax.all_to_all(outgoing, ("ctx", "sub"), split_axis=1, concat_axis=1, tiled=True)
    owners = pairs.T.reshape(-1)
    select = (jnp.arange(spans, dtype=jnp.int32)[:, None] == owners[None, :]).astype(jnp.float32)
    summed = jnp.dot(
        select,
        incoming.reshape(2 * spans, stripe * features),
        precision=lax.Precision.HIGHEST,
        preferred_element_type=jnp.float32,
    )
    at_home = lax.all_to_all(
        summed.reshape(spans, stripe, features),
        ("ctx", "sub"),
        split_axis=0,
        concat_axis=0,
        tiled=True,
    )
    at_home = at_home.reshape(rows_here, heads_here, 2 * head_dim)
    grad_keys = key_local + at_home[:, :, :head_dim]
    grad_values = value_local + at_home[:, :, head_dim:]
    grad_queries = query_sum.reshape(rows_here, heads_here * grouped, head_dim)
    return (grad_queries, grad_keys, grad_values)


def solution(mesh):
    return jax.shard_map(
        functools.partial(body, mesh.shape["ctx"], mesh.shape["sub"]),
        mesh=mesh,
        in_specs=(
            P(("groups", "ctx", "sub"), "head", None),
            P(("groups", "ctx", "sub"), "head", None),
            P(("groups", "ctx", "sub"), "head", None),
            P(("groups", "ctx", "sub"), "head", None),
            P(("groups", "ctx", "sub"), "head"),
            P(("groups", "ctx", "sub"), "head"),
            P(("groups", "ctx", "sub")),
            P("groups", None),
        ),
        out_specs=(
            P(("groups", "ctx", "sub"), "head", None),
            P(("groups", "ctx", "sub"), "head", None),
            P(("groups", "ctx", "sub"), "head", None),
        ),
        check_vma=False,
    )
```

```python
import functools
import math

import jax
import jax.numpy as jnp
from jax import lax
from jax.experimental import pallas as pl
from jax.experimental.pallas import tpu as pltpu
from jax.sharding import PartitionSpec as P

BF = jnp.bfloat16
F32 = jnp.float32
MESH = pl.DeviceIdType.MESH


def pieces_of(x):
    hi = x.astype(BF)
    rest = x - hi.astype(F32)
    mid = rest.astype(BF)
    lo = (rest - mid.astype(F32)).astype(BF)
    return hi, mid, lo


def kernel(
    dims,
    pairs_ref, docs_hbm, lse_hbm, delta_hbm, keys_hbm, vals_hbm, q_hbm, up_hbm,
    dq_vm, dk_ref, dv_ref,
    docs_ref, lse_ref, delta_ref, keys_ref, vals_ref, q_vm, up_vm,
    qa, da, bias, kfar, vfar, kloc, vloc, probs,
    dk_loc, dv_loc, kv, send_a, recv_a, send_b, recv_b,
    in_sem, z_send, p_send, z_recv, p_recv, a_send, a_recv, b_send, b_recv,
):
    zs, ss, rows, kvh, grp, hd = dims
    spans = zs * ss
    stripe = rows // spans
    chunks = 2 * kvh
    factor = hd ** -0.5
    scale2 = factor * math.log2(math.e)
    z = lax.axis_index("ctx")
    s = lax.axis_index("sub")
    me = z * ss + s
    other = 1 - s
    mine = s * zs + z
    nt = (((1,), (1,)), ((), ()))
    tn = (((0,), (0,)), ((), ()))

    barrier = pltpu.get_barrier_semaphore()

    def greet(dz, ds):
        pl.semaphore_signal(barrier, inc=1, device_id={"ctx": dz, "sub": ds}, device_id_type=MESH)

    greet(z, other)

    @pl.when(z > 0)
    def _():
        greet(z - 1, s)

    @pl.when(z < zs - 1)
    def _():
        greet(z + 1, s)

    ins = [
        pltpu.make_async_copy(src, dst, in_sem.at[i])
        for i, (src, dst) in enumerate((
            (keys_hbm, keys_ref), (vals_hbm, vals_ref), (lse_hbm, lse_ref), (delta_hbm, delta_ref),
            (docs_hbm, docs_ref), (q_hbm, q_vm), (up_hbm, up_vm),
        ))
    ]
    for c in ins:
        c.start()

    pick_t = lax.broadcasted_iota(jnp.int32, (rows, rows * kvh), 0)
    pick_r = lax.broadcasted_iota(jnp.int32, (rows, rows * kvh), 1)
    for part, ref in enumerate((keys_ref, vals_ref)):
        ins[part].wait()
        for g in range(kvh):
            pick = jnp.where(pick_r == pick_t * kvh + g, 1.0, 0.0).astype(BF)
            took = jnp.dot(pick, ref[...], preferred_element_type=F32)
            kv[g * 2 + part][mine] = took.astype(BF)

    ends = jnp.where(z > 0, 1, 0) + jnp.where(z < zs - 1, 1, 0)
    pl.semaphore_wait(barrier, 1 + ends)

    def to_line(c, slot, from_z, dz, way):
        return pltpu.make_async_remote_copy(
            src_ref=kv[c].at[slot], dst_ref=kv[c].at[slot],
            send_sem=z_send.at[c, way], recv_sem=z_recv.at[c, from_z],
            device_id={"ctx": dz, "sub": s}, device_id_type=MESH)

    def to_partner(c, slots):
        return pltpu.make_async_remote_copy(
            src_ref=kv[c].at[slots], dst_ref=kv[c].at[slots],
            send_sem=p_send.at[c], recv_sem=p_recv.at[c],
            device_id={"ctx": z, "sub": other}, device_id_type=MESH)

    def own_step(c):
        @pl.when(z < zs - 1)
        def _():
            to_line(c, mine, z, z + 1, 0).start()

        @pl.when(z > 0)
        def _():
            to_line(c, mine, z, z - 1, 1).start()

        to_partner(c, mine).start()

    def relay_step(c, j):
        @pl.when(z >= j)
        def _():
            slot = mine - j
            to_line(c, slot, z - j, z, 0).wait_recv()

            @pl.when(z < zs - 1)
            def _():
                to_line(c, slot, z - j, z + 1, 0).start()

            to_partner(c, slot).start()

        @pl.when(z + j < zs)
        def _():
            slot = mine + j
            to_line(c, slot, z + j, z, 1).wait_recv()

            @pl.when(z > 0)
            def _():
                to_line(c, slot, z + j, z - 1, 1).start()

            to_partner(c, slot).start()

    def line_sent(c):
        for at in range(zs):
            @pl.when(z == at)
            def _():
                if at < zs - 1:
                    to_line(c, pl.ds(0, at + 1), at, z, 0).wait_send()
                if at > 0:
                    to_line(c, pl.ds(0, zs - at), at, z, 1).wait_send()

        to_partner(c, pl.ds(0, zs)).wait_send()

    for c in range(chunks):
        own_step(c)

    for c in ins[2:5]:
        c.wait()
    pos_t = lax.broadcasted_iota(jnp.int32, (rows, rows), 0)
    pos_u = lax.broadcasted_iota(jnp.int32, (rows, rows), 1)
    doc_u = jnp.broadcast_to(docs_ref[...].astype(F32), (rows, rows))
    doc_t = doc_u.T
    bias[...] = jnp.where((pos_t >= pos_u) & (doc_u == doc_t), 0.0, -3e38)

    heads = kvh * grp
    put_h = lax.broadcasted_iota(jnp.int32, (heads, hd), 0)
    put_l = lax.broadcasted_iota(jnp.int32, (heads, hd), 1)

    def lanes_of(x):
        total = jnp.zeros((rows, hd), F32)
        for i, piece in enumerate(pieces_of(x)):
            place = jnp.where(put_l == put_h + i * heads, 1.0, 0.0).astype(BF)
            total = total + lax.dot_general(piece, place, tn, preferred_element_type=F32)
        return total.astype(BF)

    lse_l = lanes_of(lse_ref[...] * (hd ** 0.5))
    del_l = lanes_of(delta_ref[...])
    row_h = lax.broadcasted_iota(jnp.int32, (grp, hd), 0)
    row_l = lax.broadcasted_iota(jnp.int32, (grp, hd), 1)
    used = lax.broadcasted_iota(jnp.int32, (rows, hd), 1) < 3 * heads
    neg = jnp.where(used, -1.0, 0.0).astype(BF)
    kloc[:, hd:] = neg
    vloc[:, hd:] = neg
    for j in range(2):
        js = slice(j * rows, (j + 1) * rows)
        kfar[js, hd:] = neg
        vfar[js, hd:] = neg
    for c in ins[5:]:
        c.wait()

    def near(g):
        head = row_h + g * grp
        hit = (row_l == head) | (row_l == head + heads) | (row_l == head + 2 * heads)
        keep = jnp.where(hit, 1.0, 0.0).astype(BF)
        sl = pl.ds(g * grp, grp)
        qa[g, :, :hd] = q_vm[:, sl, :].reshape(rows * grp, hd)
        da[g, :, :hd] = up_vm[:, sl, :].reshape(rows * grp, hd)
        qa[g, :, hd:] = (lse_l[:, None, :] * keep[None]).reshape(rows * grp, hd)
        da[g, :, hd:] = (del_l[:, None, :] * keep[None]).reshape(rows * grp, hd)
        kloc[:, :hd] = kv[g * 2][mine]
        vloc[:, :hd] = kv[g * 2 + 1][mine]
        x = lax.dot_general(qa[g], kloc[...], nt, preferred_element_type=F32)
        y = lax.dot_general(da[g], vloc[...], nt, preferred_element_type=F32)
        x = (x.reshape(rows, grp, rows) + bias[...][:, None, :]).reshape(rows * grp, rows)
        p = jnp.exp2(x * scale2)
        ds_low = (p * y).astype(BF)
        p_low = p.astype(BF)
        dq = jnp.dot(ds_low, kloc[:, :hd], preferred_element_type=F32)
        dk_loc[g] = lax.dot_general(ds_low, qa[g, :, :hd], tn, preferred_element_type=F32)
        dv_loc[g] = lax.dot_general(p_low, da[g, :, :hd], tn, preferred_element_type=F32)
        dq_vm[:, sl, :] = dq.reshape(rows, grp, hd)

    def listed(c, dst):
        for j in range(2):
            span = pairs_ref[j, me]
            dst[pl.ds(j * rows, rows), :hd] = kv[c][lax.rem(span, ss) * zs + lax.div(span, ss)]

    def peer_of(off):
        d = lax.rem(me + off, spans)
        return d, {"ctx": d // ss, "sub": lax.rem(d, ss)}

    def give(c, total):
        for j in range(2):
            part = total[j * rows:(j + 1) * rows].astype(BF)
            send_a[c * spans:(c + 1) * spans, j] = part.reshape(spans, stripe, hd)
        recv_a[c * spans + me] = send_a[c * spans + me]
        for off in range(1, spans):
            d, at = peer_of(off)
            pltpu.make_async_remote_copy(
                src_ref=send_a.at[c * spans + d], dst_ref=recv_a.at[c * spans + me],
                send_sem=a_send.at[0], recv_sem=a_recv.at[c],
                device_id=at, device_id_type=MESH).start()

    def far_keys(g):
        listed(g * 2, kfar)
        x = lax.dot_general(qa[g], kfar[...], nt, preferred_element_type=F32)
        p = jnp.exp2(x * scale2)
        probs[...] = p
        give(g * 2 + 1, lax.dot_general(p.astype(BF), da[g, :, :hd], tn, preferred_element_type=F32))

    def far_vals(g):
        listed(g * 2 + 1, vfar)
        y = lax.dot_general(da[g], vfar[...], nt, preferred_element_type=F32)
        ds_low = (probs[...] * y).astype(BF)
        give(g * 2, lax.dot_general(ds_low, qa[g, :, :hd], tn, preferred_element_type=F32))
        dq = jnp.dot(ds_low, kfar[:, :hd], preferred_element_type=F32).reshape(rows, grp, hd)
        sl = pl.ds(g * grp, grp)
        dq_vm[:, sl, :] = (dq_vm[:, sl, :] + dq) * factor

    def many(ref, first, count, send_sem, recv_sem):
        return pltpu.make_async_remote_copy(
            src_ref=ref.at[pl.ds(first, count)], dst_ref=ref.at[pl.ds(first, count)],
            send_sem=send_sem, recv_sem=recv_sem,
            device_id={"ctx": z, "sub": other}, device_id_type=MESH)

    def combine(c):
        many(recv_a, c * spans, spans - 1, a_send.at[0], a_recv.at[c]).wait_recv()

        def owner(o, _):
            total = jnp.zeros((stripe, hd), F32)
            for src in range(spans):
                for j in range(2):
                    got = recv_a[c * spans + src, j].astype(F32)
                    total = total + jnp.where(pairs_ref[j, src] == o, got, 0.0)
            send_b[c * spans + o] = total.astype(BF)
            return 0

        lax.fori_loop(0, spans, owner, 0)
        recv_b[c * spans + me] = send_b[c * spans + me]
        for off in range(1, spans):
            d, at = peer_of(off)
            pltpu.make_async_remote_copy(
                src_ref=send_b.at[c * spans + d], dst_ref=recv_b.at[c * spans + me],
                send_sem=b_send.at[0], recv_sem=b_recv.at[c],
                device_id=at, device_id_type=MESH).start()

    def finish(c):
        g, part = c // 2, c % 2
        many(recv_b, c * spans, spans - 1, b_send.at[0], b_recv.at[c]).wait_recv()
        home = recv_b[c * spans:(c + 1) * spans].reshape(rows, hd).astype(F32)
        at = pl.ds(g, rows, stride=kvh)
        if part == 0:
            dk_ref[at, :] = (dk_loc[g] + home) * factor
        else:
            dv_ref[at, :] = dv_loc[g] + home

    def partner_wait(c):
        to_partner(c, pl.ds(other * zs, zs)).wait_recv()

    for g in range(kvh):
        near(g)
        relay_step(g * 2, 1)
        relay_step(g * 2 + 1, 1)
    for j in range(2, zs - 1):
        for c in range(chunks):
            relay_step(c, j)

    last = zs - 1
    if last > 1:
        relay_step(0, last)
        relay_step(1, last)
    for c in range(chunks):
        partner_wait(c)
        (far_keys if c % 2 == 0 else far_vals)(c // 2)
        if last > 1 and c + 2 < chunks:
            relay_step(c + 2, last)
    order = [g * 2 + part for g in range(kvh) for part in (1, 0)]
    for c in order:
        combine(c)
    for c in order:
        finish(c)
    for c in range(chunks):
        line_sent(c)
    many(send_a, 0, chunks * (spans - 1), a_send.at[0], a_recv.at[0]).wait_send()
    many(send_b, 0, chunks * (spans - 1), b_send.at[0], b_recv.at[0]).wait_send()


def tail_kernel(dq_vm, dk_vm, dv_vm, dq_out, dk_out, dv_out, sems):
    copies = [
        pltpu.make_async_copy(src, dst, sems.at[i])
        for i, (src, dst) in enumerate(((dq_vm, dq_out), (dk_vm, dk_out), (dv_vm, dv_out)))
    ]
    for c in copies:
        c.start()
    for c in copies:
        c.wait()


def written(dq, dk, dv):
    return pl.pallas_call(
        tail_kernel,
        out_shape=tuple(jax.ShapeDtypeStruct(x.shape, F32) for x in (dq, dk, dv)),
        in_specs=[pl.BlockSpec(memory_space=pltpu.VMEM)] * 3,
        out_specs=(pl.BlockSpec(memory_space=pltpu.HBM),) * 3,
        scratch_shapes=[pltpu.SemaphoreType.DMA((3,))],
        compiler_params=pltpu.CompilerParams(vmem_limit_bytes=4 * 1024 * 1024),
        name="write_out",
    )(dq, dk, dv)


def fused(zs, ss, queries, keys, values, grad_out, row_lse, row_delta, doc_ids, pairs):
    rows, qh, hd = queries.shape
    kvh = keys.shape[1]
    grp = qh // kvh
    spans = zs * ss
    stripe = rows // spans
    chunks = 2 * kvh
    vm = pl.BlockSpec(memory_space=pltpu.VMEM)
    sm = pl.BlockSpec(memory_space=pltpu.SMEM)
    hbm = pl.BlockSpec(memory_space=pltpu.HBM)
    dma = pltpu.SemaphoreType.DMA
    dq, dk, dv = pl.pallas_call(
        functools.partial(kernel, (zs, ss, rows, kvh, grp, hd)),
        out_shape=(
            pltpu.VMEM((rows, qh, hd), F32),
            pltpu.VMEM((rows * kvh, hd), F32),
            pltpu.VMEM((rows * kvh, hd), F32),
        ),
        in_specs=[sm, hbm, hbm, hbm, hbm, hbm, hbm, hbm],
        out_specs=(vm, vm, vm),
        scratch_shapes=[
            pltpu.VMEM((1, rows), jnp.int32),
            pltpu.VMEM((qh, rows), F32),
            pltpu.VMEM((qh, rows), F32),
            pltpu.VMEM((rows * kvh, hd), BF),
            pltpu.VMEM((rows * kvh, hd), BF),
            pltpu.VMEM((rows, qh, hd), BF),
            pltpu.VMEM((rows, qh, hd), BF),
            pltpu.VMEM((kvh, rows * grp, 2 * hd), BF),
            pltpu.VMEM((kvh, rows * grp, 2 * hd), BF),
            pltpu.VMEM((rows, rows), F32),
            pltpu.VMEM((2 * rows, 2 * hd), BF),
            pltpu.VMEM((2 * rows, 2 * hd), BF),
            pltpu.VMEM((rows, 2 * hd), BF),
            pltpu.VMEM((rows, 2 * hd), BF),
            pltpu.VMEM((rows * grp, 2 * rows), F32),
            pltpu.VMEM((kvh, rows, hd), F32),
            pltpu.VMEM((kvh, rows, hd), F32),
            [pltpu.VMEM((spans, rows, hd), BF) for _ in range(chunks)],
            pltpu.VMEM((chunks * spans, 2, stripe, hd), BF),
            pltpu.VMEM((chunks * spans, 2, stripe, hd), BF),
            pltpu.VMEM((chunks * spans, stripe, hd), BF),
            pltpu.VMEM((chunks * spans, stripe, hd), BF),
            dma((7,)),
            dma((chunks, 2)),
            dma((chunks,)),
            dma((chunks, zs)),
            dma((chunks,)),
            dma((1,)),
            dma((chunks,)),
            dma((1,)),
            dma((chunks,)),
        ],
        compiler_params=pltpu.CompilerParams(collective_id=0, has_side_effects=True),
        name="span_grads",
    )(
        pairs.T, doc_ids.reshape(1, rows), row_lse.T, row_delta.T,
        keys.reshape(rows * kvh, hd), values.reshape(rows * kvh, hd), queries, grad_out,
    )
    dq, dk, dv = written(dq, dk, dv)
    return dq, dk.reshape(rows, kvh, hd), dv.reshape(rows, kvh, hd)


QH = 64
KVH = 4


def block_terms(query_blk, upstream, log_norm, row_terms, key_blk, value_blk, allowed, factor):
    scores = (
        jnp.einsum("tghd,kgd->tghk", query_blk, key_blk, preferred_element_type=jnp.float32)
        * factor
    )
    probs = jnp.exp(scores - log_norm[..., None])
    if allowed is not None:
        probs = jnp.where(allowed[:, None, None, :], probs, 0.0)
    grad_probs = jnp.einsum(
        "tghd,kgd->tghk", upstream, value_blk, preferred_element_type=jnp.float32
    )
    grad_scores = probs * (grad_probs - row_terms[..., None])
    probs_low = probs.astype(jnp.bfloat16)
    scores_low = grad_scores.astype(jnp.bfloat16)
    grad_val = jnp.einsum("tghk,tghd->kgd", probs_low, upstream, preferred_element_type=jnp.float32)
    grad_key = (
        jnp.einsum("tghk,tghd->kgd", scores_low, query_blk, preferred_element_type=jnp.float32)
        * factor
    )
    grad_query = (
        jnp.einsum("tghk,kgd->tghd", scores_low, key_blk, preferred_element_type=jnp.float32)
        * factor
    )
    return (grad_query, grad_key, grad_val)


def body(zs, ss, queries, keys, values, grad_out, row_lse, row_delta, doc_ids, pairs):
    grp = queries.shape[1] // keys.shape[1]
    if (
        ss == 2
        and queries.shape[0] % (16 * zs * ss) == 0
        and grp % 16 == 0
        and 3 * queries.shape[1] <= queries.shape[2]
    ):
        return fused(
            zs, ss, queries, keys, values, grad_out, row_lse, row_delta, doc_ids, pairs
        )
    rows_here = queries.shape[0]
    heads_here = keys.shape[1]
    head_dim = keys.shape[2]
    grouped = QH // KVH
    factor = head_dim ** (-0.5)
    spans = lax.axis_size(("ctx", "sub"))
    stripe = rows_here // spans
    query_blk = queries.reshape(rows_here, heads_here, grouped, head_dim)
    upstream = grad_out.reshape(rows_here, heads_here, grouped, head_dim)
    log_norm = row_lse.reshape(rows_here, heads_here, grouped)
    row_terms = row_delta.reshape(rows_here, heads_here, grouped)
    positions = jnp.arange(rows_here, dtype=jnp.int32)
    allowed = (positions[:, None] >= positions[None, :]) & (doc_ids[:, None] == doc_ids[None, :])
    query_sum, key_local, value_local = block_terms(
        query_blk, upstream, log_norm, row_terms, keys, values, allowed, factor
    )
    stacked = jnp.concatenate([keys, values], axis=2).reshape(rows_here, heads_here * 2 * head_dim)
    features = stacked.shape[1]
    spread = lax.all_to_all(
        stacked.reshape(spans, stripe, features),
        ("ctx", "sub"),
        split_axis=0,
        concat_axis=0,
        tiled=True,
    )
    wanted = jnp.take(spread, pairs.T, axis=0)
    remote = lax.all_to_all(
        wanted, ("ctx", "sub"), split_axis=1, concat_axis=1, tiled=True
    ).reshape(2, rows_here, features)
    remote = remote.reshape(2, rows_here, heads_here, 2 * head_dim)
    returned = []
    for which in range(2):
        far_keys = remote[which, :, :, :head_dim]
        far_values = remote[which, :, :, head_dim:]
        query_part, key_part, value_part = block_terms(
            query_blk, upstream, log_norm, row_terms, far_keys, far_values, None, factor
        )
        query_sum = query_sum + query_part
        returned.append(
            jnp.concatenate([key_part, value_part], axis=2).reshape(rows_here, features)
        )
    outgoing = jnp.stack(returned).reshape(2, spans, stripe, features)
    incoming = lax.all_to_all(outgoing, ("ctx", "sub"), split_axis=1, concat_axis=1, tiled=True)
    owners = pairs.T.reshape(-1)
    select = (jnp.arange(spans, dtype=jnp.int32)[:, None] == owners[None, :]).astype(jnp.float32)
    summed = jnp.dot(
        select,
        incoming.reshape(2 * spans, stripe * features),
        precision=lax.Precision.HIGHEST,
        preferred_element_type=jnp.float32,
    )
    at_home = lax.all_to_all(
        summed.reshape(spans, stripe, features),
        ("ctx", "sub"),
        split_axis=0,
        concat_axis=0,
        tiled=True,
    )
    at_home = at_home.reshape(rows_here, heads_here, 2 * head_dim)
    grad_keys = key_local + at_home[:, :, :head_dim]
    grad_values = value_local + at_home[:, :, head_dim:]
    grad_queries = query_sum.reshape(rows_here, heads_here * grouped, head_dim)
    return (grad_queries, grad_keys, grad_values)


def solution(mesh):
    return jax.shard_map(
        functools.partial(body, mesh.shape["ctx"], mesh.shape["sub"]),
        mesh=mesh,
        in_specs=(
            P(("groups", "ctx", "sub"), "head", None),
            P(("groups", "ctx", "sub"), "head", None),
            P(("groups", "ctx", "sub"), "head", None),
            P(("groups", "ctx", "sub"), "head", None),
            P(("groups", "ctx", "sub"), "head"),
            P(("groups", "ctx", "sub"), "head"),
            P(("groups", "ctx", "sub")),
            P("groups", None),
        ),
        out_specs=(
            P(("groups", "ctx", "sub"), "head", None),
            P(("groups", "ctx", "sub"), "head", None),
            P(("groups", "ctx", "sub"), "head", None),
        ),
        check_vma=False,
    )
```

```python
import functools
import math

import jax
import jax.numpy as jnp
from jax import lax
from jax.experimental import pallas as pl
from jax.experimental.pallas import tpu as pltpu
from jax.sharding import PartitionSpec as P

BF = jnp.bfloat16
F32 = jnp.float32
MESH = pl.DeviceIdType.MESH


def pieces_of(x):
    hi = x.astype(BF)
    rest = x - hi.astype(F32)
    mid = rest.astype(BF)
    lo = (rest - mid.astype(F32)).astype(BF)
    return hi, mid, lo


def kernel(
    dims,
    pairs_ref, docs_hbm, lse_hbm, delta_hbm, keys_hbm, vals_hbm, q_hbm, up_hbm,
    dq_vm, dk_ref, dv_ref,
    docs_ref, lse_ref, delta_ref, keys_ref, vals_ref, q_vm, up_vm,
    qa, da, bias, kfar, vfar, kloc, vloc, wide,
    dk_loc, dv_loc, kv, send_a, recv_a, send_b, recv_b,
    in_sem, z_send, p_send, z_recv, p_recv, a_send, a_recv, b_send, b_recv,
):
    zs, ss, rows, kvh, grp, hd = dims
    spans = zs * ss
    stripe = rows // spans
    chunks = 2 * kvh
    factor = hd ** -0.5
    scale2 = factor * math.log2(math.e)
    z = lax.axis_index("ctx")
    s = lax.axis_index("sub")
    me = z * ss + s
    other = 1 - s
    mine = s * zs + z
    nt = (((1,), (1,)), ((), ()))
    tn = (((0,), (0,)), ((), ()))
    direct = [hop for hop in (2, 1) if hop < zs]

    barrier = pltpu.get_barrier_semaphore()

    def greet(dz, ds):
        pl.semaphore_signal(barrier, inc=1, device_id={"ctx": dz, "sub": ds}, device_id_type=MESH)

    greet(z, other)

    for hop in direct:
        @pl.when(z >= hop)
        def _():
            greet(z - hop, s)

        @pl.when(z + hop < zs)
        def _():
            greet(z + hop, s)

    ins = [
        pltpu.make_async_copy(src, dst, in_sem.at[i])
        for i, (src, dst) in enumerate((
            (keys_hbm, keys_ref), (vals_hbm, vals_ref), (lse_hbm, lse_ref), (delta_hbm, delta_ref),
            (docs_hbm, docs_ref), (q_hbm, q_vm), (up_hbm, up_vm),
        ))
    ]
    for c in ins[:5]:
        c.start()
    for part, ref in enumerate((keys_ref, vals_ref)):
        ins[part].wait()
        wide[part] = ref[...].astype(F32)
        for g in range(kvh):
            kv[g * 2 + part][mine] = wide[part, pl.ds(g, rows, stride=kvh), :].astype(BF)

    ends = sum(jnp.where(z >= hop, 1, 0) + jnp.where(z + hop < zs, 1, 0) for hop in direct)
    pl.semaphore_wait(barrier, 1 + ends)

    def to_line(c, slot, from_z, dz, way):
        return pltpu.make_async_remote_copy(
            src_ref=kv[c].at[slot], dst_ref=kv[c].at[slot],
            send_sem=z_send.at[c, way], recv_sem=z_recv.at[c, from_z],
            device_id={"ctx": dz, "sub": s}, device_id_type=MESH)

    def to_partner(c, slots):
        return pltpu.make_async_remote_copy(
            src_ref=kv[c].at[slots], dst_ref=kv[c].at[slots],
            send_sem=p_send.at[c], recv_sem=p_recv.at[c],
            device_id={"ctx": z, "sub": other}, device_id_type=MESH)

    def own_step(c):
        for hop in direct:
            @pl.when(z + hop < zs)
            def _():
                to_line(c, mine, z, z + hop, 0).start()

            @pl.when(z >= hop)
            def _():
                to_line(c, mine, z, z - hop, 1).start()

        to_partner(c, mine).start()

    def relay_step(c, j):
        @pl.when(z >= j)
        def _():
            slot = mine - j
            to_line(c, slot, z - j, z, 0).wait_recv()

            @pl.when((z < zs - 1) & (j >= len(direct)))
            def _():
                to_line(c, slot, z - j, z + 1, 0).start()

            to_partner(c, slot).start()

        @pl.when(z + j < zs)
        def _():
            slot = mine + j
            to_line(c, slot, z + j, z, 1).wait_recv()

            @pl.when((z > 0) & (j >= len(direct)))
            def _():
                to_line(c, slot, z + j, z - 1, 1).start()

            to_partner(c, slot).start()

    def line_sent(c):
        for at in range(zs):
            @pl.when(z == at)
            def _():
                for way, behind in enumerate((at, zs - 1 - at)):
                    ahead = zs - 1 - behind
                    count = min(ahead, len(direct))
                    if ahead > 0:
                        count += max(0, behind - len(direct) + 1)
                        to_line(c, pl.ds(0, count), at, z, way).wait_send()

        to_partner(c, pl.ds(0, zs)).wait_send()

    for c in range(chunks):
        own_step(c)
    for c in ins[5:]:
        c.start()

    for c in ins[2:5]:
        c.wait()
    pos_t = lax.broadcasted_iota(jnp.int32, (rows, rows), 0)
    pos_u = lax.broadcasted_iota(jnp.int32, (rows, rows), 1)
    doc_u = jnp.broadcast_to(docs_ref[...].astype(F32), (rows, rows))
    doc_t = doc_u.T
    bias[...] = jnp.where((pos_t >= pos_u) & (doc_u == doc_t), 0.0, -3e38)

    heads = kvh * grp
    put_h = lax.broadcasted_iota(jnp.int32, (heads, hd), 0)
    put_l = lax.broadcasted_iota(jnp.int32, (heads, hd), 1)

    def lanes_of(x):
        total = jnp.zeros((rows, hd), F32)
        for i, piece in enumerate(pieces_of(x)):
            place = jnp.where(put_l == put_h + i * heads, 1.0, 0.0).astype(BF)
            total = total + lax.dot_general(piece, place, tn, preferred_element_type=F32)
        return total.astype(BF)

    lse_l = lanes_of(lse_ref[...] * (hd ** 0.5))
    del_l = lanes_of(delta_ref[...])
    row_h = lax.broadcasted_iota(jnp.int32, (grp, hd), 0)
    row_l = lax.broadcasted_iota(jnp.int32, (grp, hd), 1)
    used = lax.broadcasted_iota(jnp.int32, (rows, hd), 1) < 3 * heads
    neg = jnp.where(used, -1.0, 0.0).astype(BF)
    kloc[:, hd:] = neg
    vloc[:, hd:] = neg
    for j in range(2):
        js = slice(j * rows, (j + 1) * rows)
        kfar[js, hd:] = neg
        vfar[js, hd:] = neg
    for c in ins[5:]:
        c.wait()

    def near(g):
        head = row_h + g * grp
        hit = (row_l == head) | (row_l == head + heads) | (row_l == head + 2 * heads)
        keep = jnp.where(hit, 1.0, 0.0).astype(BF)
        sl = pl.ds(g * grp, grp)
        qa[g, :, :hd] = q_vm[:, sl, :].reshape(rows * grp, hd)
        da[g, :, :hd] = up_vm[:, sl, :].reshape(rows * grp, hd)
        qa[g, :, hd:] = (lse_l[:, None, :] * keep[None]).reshape(rows * grp, hd)
        da[g, :, hd:] = (del_l[:, None, :] * keep[None]).reshape(rows * grp, hd)
        kloc[:, :hd] = kv[g * 2][mine]
        vloc[:, :hd] = kv[g * 2 + 1][mine]
        x = lax.dot_general(qa[g], kloc[...], nt, preferred_element_type=F32)
        y = lax.dot_general(da[g], vloc[...], nt, preferred_element_type=F32)
        x = (x.reshape(rows, grp, rows) + bias[...][:, None, :]).reshape(rows * grp, rows)
        p = jnp.exp2(x * scale2)
        ds_low = (p * y).astype(BF)
        p_low = p.astype(BF)
        dq = jnp.dot(ds_low, kloc[:, :hd], preferred_element_type=F32)
        dk_loc[g] = lax.dot_general(ds_low, qa[g, :, :hd], tn, preferred_element_type=F32)
        dv_loc[g] = lax.dot_general(p_low, da[g, :, :hd], tn, preferred_element_type=F32)
        dq_vm[:, sl, :] = dq.reshape(rows, grp, hd)

    def listed(c, dst):
        for j in range(2):
            span = pairs_ref[j, me]
            dst[pl.ds(j * rows, rows), :hd] = kv[c][lax.rem(span, ss) * zs + lax.div(span, ss)]

    def peer_of(off):
        d = lax.rem(me + off, spans)
        return d, {"ctx": d // ss, "sub": lax.rem(d, ss)}

    def give(c, total):
        for j in range(2):
            part = total[j * rows:(j + 1) * rows].astype(BF)
            send_a[c * spans:(c + 1) * spans, j] = part.reshape(spans, stripe, hd)
        recv_a[c * spans + me] = send_a[c * spans + me]
        for off in range(1, spans):
            d, at = peer_of(off)
            pltpu.make_async_remote_copy(
                src_ref=send_a.at[c * spans + d], dst_ref=recv_a.at[c * spans + me],
                send_sem=a_send.at[0], recv_sem=a_recv.at[c],
                device_id=at, device_id_type=MESH).start()

    def far(g):
        listed(g * 2, kfar)
        listed(g * 2 + 1, vfar)
        x = lax.dot_general(qa[g], kfar[...], nt, preferred_element_type=F32)
        y = lax.dot_general(da[g], vfar[...], nt, preferred_element_type=F32)
        p = jnp.exp2(x * scale2)
        ds_low = (p * y).astype(BF)
        dq = jnp.dot(ds_low, kfar[:, :hd], preferred_element_type=F32).reshape(rows, grp, hd)
        dk = lax.dot_general(ds_low, qa[g, :, :hd], tn, preferred_element_type=F32)
        dv = lax.dot_general(p.astype(BF), da[g, :, :hd], tn, preferred_element_type=F32)
        sl = pl.ds(g * grp, grp)
        dq_vm[:, sl, :] = (dq_vm[:, sl, :] + dq) * factor
        give(g * 2 + 1, dv)
        give(g * 2, dk)

    def many(ref, first, count, send_sem, recv_sem):
        return pltpu.make_async_remote_copy(
            src_ref=ref.at[pl.ds(first, count)], dst_ref=ref.at[pl.ds(first, count)],
            send_sem=send_sem, recv_sem=recv_sem,
            device_id={"ctx": z, "sub": other}, device_id_type=MESH)

    def combine(c):
        many(recv_a, c * spans, spans - 1, a_send.at[0], a_recv.at[c]).wait_recv()

        def owner(o, _):
            total = jnp.zeros((stripe, hd), F32)
            for src in range(spans):
                for j in range(2):
                    got = recv_a[c * spans + src, j].astype(F32)
                    total = total + jnp.where(pairs_ref[j, src] == o, got, 0.0)
            send_b[c * spans + o] = total.astype(BF)
            return 0

        lax.fori_loop(0, spans, owner, 0)
        recv_b[c * spans + me] = send_b[c * spans + me]
        for off in range(1, spans):
            d, at = peer_of(off)
            pltpu.make_async_remote_copy(
                src_ref=send_b.at[c * spans + d], dst_ref=recv_b.at[c * spans + me],
                send_sem=b_send.at[0], recv_sem=b_recv.at[c],
                device_id=at, device_id_type=MESH).start()

    def finish(c):
        g, part = c // 2, c % 2
        many(recv_b, c * spans, spans - 1, b_send.at[0], b_recv.at[c]).wait_recv()
        home = recv_b[c * spans:(c + 1) * spans].reshape(rows, hd).astype(F32)
        at = pl.ds(g, rows, stride=kvh)
        if part == 0:
            dk_ref[at, :] = (dk_loc[g] + home) * factor
        else:
            dv_ref[at, :] = dv_loc[g] + home

    def partner_wait(c):
        to_partner(c, pl.ds(other * zs, zs)).wait_recv()

    last = zs - 1
    for g in range(kvh):
        near(g)
        for c in ([0] if g == 0 else []) + (list(range(1, chunks)) if g == kvh - 1 else []):
            for j in range(1, min(last, len(direct) + 1)):
                relay_step(c, j)
    for j in range(len(direct) + 1, last):
        for c in range(chunks):
            relay_step(c, j)
    for g in range(kvh):
        for c in (g * 2, g * 2 + 1):
            relay_step(c, last)
        for c in (g * 2, g * 2 + 1):
            partner_wait(c)
        far(g)
    order = [g * 2 + part for g in range(kvh) for part in (1, 0)]
    for c in order:
        combine(c)
    for c in order:
        finish(c)
    for c in range(chunks):
        line_sent(c)
    many(send_a, 0, chunks * (spans - 1), a_send.at[0], a_recv.at[0]).wait_send()
    many(send_b, 0, chunks * (spans - 1), b_send.at[0], b_recv.at[0]).wait_send()


def tail_kernel(dq_vm, dk_vm, dv_vm, dq_out, dk_out, dv_out, sems):
    copies = [
        pltpu.make_async_copy(src, dst, sems.at[i])
        for i, (src, dst) in enumerate(((dq_vm, dq_out), (dk_vm, dk_out), (dv_vm, dv_out)))
    ]
    for c in copies:
        c.start()
    for c in copies:
        c.wait()


def written(dq, dk, dv):
    return pl.pallas_call(
        tail_kernel,
        out_shape=tuple(jax.ShapeDtypeStruct(x.shape, F32) for x in (dq, dk, dv)),
        in_specs=[pl.BlockSpec(memory_space=pltpu.VMEM)] * 3,
        out_specs=(pl.BlockSpec(memory_space=pltpu.HBM),) * 3,
        scratch_shapes=[pltpu.SemaphoreType.DMA((3,))],
        compiler_params=pltpu.CompilerParams(vmem_limit_bytes=4 * 1024 * 1024),
        name="write_out",
    )(dq, dk, dv)


def fused(zs, ss, queries, keys, values, grad_out, row_lse, row_delta, doc_ids, pairs):
    rows, qh, hd = queries.shape
    kvh = keys.shape[1]
    grp = qh // kvh
    spans = zs * ss
    stripe = rows // spans
    chunks = 2 * kvh
    vm = pl.BlockSpec(memory_space=pltpu.VMEM)
    sm = pl.BlockSpec(memory_space=pltpu.SMEM)
    hbm = pl.BlockSpec(memory_space=pltpu.HBM)
    dma = pltpu.SemaphoreType.DMA
    dq, dk, dv = pl.pallas_call(
        functools.partial(kernel, (zs, ss, rows, kvh, grp, hd)),
        out_shape=(
            pltpu.VMEM((rows, qh, hd), F32),
            pltpu.VMEM((rows * kvh, hd), F32),
            pltpu.VMEM((rows * kvh, hd), F32),
        ),
        in_specs=[sm, hbm, hbm, hbm, hbm, hbm, hbm, hbm],
        out_specs=(vm, vm, vm),
        scratch_shapes=[
            pltpu.VMEM((1, rows), jnp.int32),
            pltpu.VMEM((qh, rows), F32),
            pltpu.VMEM((qh, rows), F32),
            pltpu.VMEM((rows * kvh, hd), BF),
            pltpu.VMEM((rows * kvh, hd), BF),
            pltpu.VMEM((rows, qh, hd), BF),
            pltpu.VMEM((rows, qh, hd), BF),
            pltpu.VMEM((kvh, rows * grp, 2 * hd), BF),
            pltpu.VMEM((kvh, rows * grp, 2 * hd), BF),
            pltpu.VMEM((rows, rows), F32),
            pltpu.VMEM((2 * rows, 2 * hd), BF),
            pltpu.VMEM((2 * rows, 2 * hd), BF),
            pltpu.VMEM((rows, 2 * hd), BF),
            pltpu.VMEM((rows, 2 * hd), BF),
            pltpu.VMEM((2, rows * kvh, hd), F32),
            pltpu.VMEM((kvh, rows, hd), F32),
            pltpu.VMEM((kvh, rows, hd), F32),
            [pltpu.VMEM((spans, rows, hd), BF) for _ in range(chunks)],
            pltpu.VMEM((chunks * spans, 2, stripe, hd), BF),
            pltpu.VMEM((chunks * spans, 2, stripe, hd), BF),
            pltpu.VMEM((chunks * spans, stripe, hd), BF),
            pltpu.VMEM((chunks * spans, stripe, hd), BF),
            dma((7,)),
            dma((chunks, 2)),
            dma((chunks,)),
            dma((chunks, zs)),
            dma((chunks,)),
            dma((1,)),
            dma((chunks,)),
            dma((1,)),
            dma((chunks,)),
        ],
        compiler_params=pltpu.CompilerParams(collective_id=0, has_side_effects=True),
        name="span_grads",
    )(
        pairs.T, doc_ids.reshape(1, rows), row_lse.T, row_delta.T,
        keys.reshape(rows * kvh, hd), values.reshape(rows * kvh, hd), queries, grad_out,
    )
    dq, dk, dv = written(dq, dk, dv)
    return dq, dk.reshape(rows, kvh, hd), dv.reshape(rows, kvh, hd)


QH = 64
KVH = 4


def block_terms(query_blk, upstream, log_norm, row_terms, key_blk, value_blk, allowed, factor):
    scores = (
        jnp.einsum("tghd,kgd->tghk", query_blk, key_blk, preferred_element_type=jnp.float32)
        * factor
    )
    probs = jnp.exp(scores - log_norm[..., None])
    if allowed is not None:
        probs = jnp.where(allowed[:, None, None, :], probs, 0.0)
    grad_probs = jnp.einsum(
        "tghd,kgd->tghk", upstream, value_blk, preferred_element_type=jnp.float32
    )
    grad_scores = probs * (grad_probs - row_terms[..., None])
    probs_low = probs.astype(jnp.bfloat16)
    scores_low = grad_scores.astype(jnp.bfloat16)
    grad_val = jnp.einsum("tghk,tghd->kgd", probs_low, upstream, preferred_element_type=jnp.float32)
    grad_key = (
        jnp.einsum("tghk,tghd->kgd", scores_low, query_blk, preferred_element_type=jnp.float32)
        * factor
    )
    grad_query = (
        jnp.einsum("tghk,kgd->tghd", scores_low, key_blk, preferred_element_type=jnp.float32)
        * factor
    )
    return (grad_query, grad_key, grad_val)


def body(zs, ss, queries, keys, values, grad_out, row_lse, row_delta, doc_ids, pairs):
    grp = queries.shape[1] // keys.shape[1]
    if (
        ss == 2
        and queries.shape[0] % (16 * zs * ss) == 0
        and grp % 16 == 0
        and 3 * queries.shape[1] <= queries.shape[2]
    ):
        return fused(
            zs, ss, queries, keys, values, grad_out, row_lse, row_delta, doc_ids, pairs
        )
    rows_here = queries.shape[0]
    heads_here = keys.shape[1]
    head_dim = keys.shape[2]
    grouped = QH // KVH
    factor = head_dim ** (-0.5)
    spans = lax.axis_size(("ctx", "sub"))
    stripe = rows_here // spans
    query_blk = queries.reshape(rows_here, heads_here, grouped, head_dim)
    upstream = grad_out.reshape(rows_here, heads_here, grouped, head_dim)
    log_norm = row_lse.reshape(rows_here, heads_here, grouped)
    row_terms = row_delta.reshape(rows_here, heads_here, grouped)
    positions = jnp.arange(rows_here, dtype=jnp.int32)
    allowed = (positions[:, None] >= positions[None, :]) & (doc_ids[:, None] == doc_ids[None, :])
    query_sum, key_local, value_local = block_terms(
        query_blk, upstream, log_norm, row_terms, keys, values, allowed, factor
    )
    stacked = jnp.concatenate([keys, values], axis=2).reshape(rows_here, heads_here * 2 * head_dim)
    features = stacked.shape[1]
    spread = lax.all_to_all(
        stacked.reshape(spans, stripe, features),
        ("ctx", "sub"),
        split_axis=0,
        concat_axis=0,
        tiled=True,
    )
    wanted = jnp.take(spread, pairs.T, axis=0)
    remote = lax.all_to_all(
        wanted, ("ctx", "sub"), split_axis=1, concat_axis=1, tiled=True
    ).reshape(2, rows_here, features)
    remote = remote.reshape(2, rows_here, heads_here, 2 * head_dim)
    returned = []
    for which in range(2):
        far_keys = remote[which, :, :, :head_dim]
        far_values = remote[which, :, :, head_dim:]
        query_part, key_part, value_part = block_terms(
            query_blk, upstream, log_norm, row_terms, far_keys, far_values, None, factor
        )
        query_sum = query_sum + query_part
        returned.append(
            jnp.concatenate([key_part, value_part], axis=2).reshape(rows_here, features)
        )
    outgoing = jnp.stack(returned).reshape(2, spans, stripe, features)
    incoming = lax.all_to_all(outgoing, ("ctx", "sub"), split_axis=1, concat_axis=1, tiled=True)
    owners = pairs.T.reshape(-1)
    select = (jnp.arange(spans, dtype=jnp.int32)[:, None] == owners[None, :]).astype(jnp.float32)
    summed = jnp.dot(
        select,
        incoming.reshape(2 * spans, stripe * features),
        precision=lax.Precision.HIGHEST,
        preferred_element_type=jnp.float32,
    )
    at_home = lax.all_to_all(
        summed.reshape(spans, stripe, features),
        ("ctx", "sub"),
        split_axis=0,
        concat_axis=0,
        tiled=True,
    )
    at_home = at_home.reshape(rows_here, heads_here, 2 * head_dim)
    grad_keys = key_local + at_home[:, :, :head_dim]
    grad_values = value_local + at_home[:, :, head_dim:]
    grad_queries = query_sum.reshape(rows_here, heads_here * grouped, head_dim)
    return (grad_queries, grad_keys, grad_values)


def solution(mesh):
    return jax.shard_map(
        functools.partial(body, mesh.shape["ctx"], mesh.shape["sub"]),
        mesh=mesh,
        in_specs=(
            P(("groups", "ctx", "sub"), "head", None),
            P(("groups", "ctx", "sub"), "head", None),
            P(("groups", "ctx", "sub"), "head", None),
            P(("groups", "ctx", "sub"), "head", None),
            P(("groups", "ctx", "sub"), "head"),
            P(("groups", "ctx", "sub"), "head"),
            P(("groups", "ctx", "sub")),
            P("groups", None),
        ),
        out_specs=(
            P(("groups", "ctx", "sub"), "head", None),
            P(("groups", "ctx", "sub"), "head", None),
            P(("groups", "ctx", "sub"), "head", None),
        ),
        check_vma=False,
    )
```

```python
import functools
import math

import jax
import jax.numpy as jnp
from jax import lax
from jax.experimental import pallas as pl
from jax.experimental.pallas import tpu as pltpu
from jax.sharding import PartitionSpec as P

BF = jnp.bfloat16
F32 = jnp.float32
MESH = pl.DeviceIdType.MESH


def pieces_of(x):
    hi = x.astype(BF)
    rest = x - hi.astype(F32)
    mid = rest.astype(BF)
    lo = (rest - mid.astype(F32)).astype(BF)
    return hi, mid, lo


def kernel(
    dims,
    pairs_hbm, docs_hbm, lse_hbm, delta_hbm, keys_hbm, vals_hbm, q_hbm, up_hbm,
    dq_vm, dk_ref, dv_ref,
    pairs_ref, docs_ref, lse_ref, delta_ref, keys_ref, vals_ref, q_vm, up_vm,
    qa, da, bias, kfar, vfar, kloc, vloc, wide, probs,
    dk_loc, dv_loc, kv, send_a, recv_a, send_b, recv_b,
    in_sem, z_send, p_send, z_recv, p_recv, a_send, a_recv, b_send, b_recv,
):
    zs, ss, rows, kvh, grp, hd = dims
    spans = zs * ss
    stripe = rows // spans
    chunks = 2 * kvh
    factor = hd ** -0.5
    scale2 = factor * math.log2(math.e)
    z = lax.axis_index("ctx")
    s = lax.axis_index("sub")
    me = z * ss + s
    other = 1 - s
    mine = s * zs + z
    nt = (((1,), (1,)), ((), ()))
    tn = (((0,), (0,)), ((), ()))

    barrier = pltpu.get_barrier_semaphore()

    def greet(dz, ds):
        pl.semaphore_signal(barrier, inc=1, device_id={"ctx": dz, "sub": ds}, device_id_type=MESH)

    greet(z, other)

    @pl.when(z > 0)
    def _():
        greet(z - 1, s)

    @pl.when(z < zs - 1)
    def _():
        greet(z + 1, s)

    ins = [
        pltpu.make_async_copy(src, dst, in_sem.at[i])
        for i, (src, dst) in enumerate((
            (keys_hbm, keys_ref), (vals_hbm, vals_ref), (lse_hbm, lse_ref), (delta_hbm, delta_ref),
            (docs_hbm, docs_ref), (pairs_hbm, pairs_ref), (q_hbm, q_vm), (up_hbm, up_vm),
        ))
    ]
    for c in ins[:6]:
        c.start()
    for part, ref in enumerate((keys_ref, vals_ref)):
        ins[part].wait()
        wide[part] = ref[...].astype(F32)
        for g in range(kvh):
            kv[g * 2 + part][mine] = wide[part, pl.ds(g, rows, stride=kvh), :].astype(BF)
    for c in ins[6:]:
        c.start()

    ends = jnp.where(z > 0, 1, 0) + jnp.where(z < zs - 1, 1, 0)
    pl.semaphore_wait(barrier, 1 + ends)

    def to_line(c, slot, from_z, dz, way):
        return pltpu.make_async_remote_copy(
            src_ref=kv[c].at[slot], dst_ref=kv[c].at[slot],
            send_sem=z_send.at[c, way], recv_sem=z_recv.at[c, from_z],
            device_id={"ctx": dz, "sub": s}, device_id_type=MESH)

    def to_partner(c, slots):
        return pltpu.make_async_remote_copy(
            src_ref=kv[c].at[slots], dst_ref=kv[c].at[slots],
            send_sem=p_send.at[c], recv_sem=p_recv.at[c],
            device_id={"ctx": z, "sub": other}, device_id_type=MESH)

    def own_step(c):
        @pl.when(z < zs - 1)
        def _():
            to_line(c, mine, z, z + 1, 0).start()

        @pl.when(z > 0)
        def _():
            to_line(c, mine, z, z - 1, 1).start()

        to_partner(c, mine).start()

    def relay_step(c, j):
        @pl.when(z >= j)
        def _():
            slot = mine - j
            to_line(c, slot, z - j, z, 0).wait_recv()

            @pl.when(z < zs - 1)
            def _():
                to_line(c, slot, z - j, z + 1, 0).start()

            to_partner(c, slot).start()

        @pl.when(z + j < zs)
        def _():
            slot = mine + j
            to_line(c, slot, z + j, z, 1).wait_recv()

            @pl.when(z > 0)
            def _():
                to_line(c, slot, z + j, z - 1, 1).start()

            to_partner(c, slot).start()

    def line_sent(c):
        for at in range(zs):
            @pl.when(z == at)
            def _():
                if at < zs - 1:
                    to_line(c, pl.ds(0, at + 1), at, z, 0).wait_send()
                if at > 0:
                    to_line(c, pl.ds(0, zs - at), at, z, 1).wait_send()

        to_partner(c, pl.ds(0, zs)).wait_send()

    for c in range(2):
        own_step(c)

    for c in ins[2:6]:
        c.wait()
    pos_t = lax.broadcasted_iota(jnp.int32, (rows, rows), 0)
    pos_u = lax.broadcasted_iota(jnp.int32, (rows, rows), 1)
    doc_u = jnp.broadcast_to(docs_ref[...].astype(F32), (rows, rows))
    doc_t = doc_u.T
    bias[...] = jnp.where((pos_t >= pos_u) & (doc_u == doc_t), 0.0, -3e38)

    heads = kvh * grp
    put_h = lax.broadcasted_iota(jnp.int32, (heads, hd), 0)
    put_l = lax.broadcasted_iota(jnp.int32, (heads, hd), 1)

    def lanes_of(x):
        total = jnp.zeros((rows, hd), F32)
        for i, piece in enumerate(pieces_of(x)):
            place = jnp.where(put_l == put_h + i * heads, 1.0, 0.0).astype(BF)
            total = total + lax.dot_general(piece, place, tn, preferred_element_type=F32)
        return total.astype(BF)

    lse_l = lanes_of(lse_ref[...] * (hd ** 0.5))
    del_l = lanes_of(delta_ref[...])
    row_h = lax.broadcasted_iota(jnp.int32, (grp, hd), 0)
    row_l = lax.broadcasted_iota(jnp.int32, (grp, hd), 1)
    used = lax.broadcasted_iota(jnp.int32, (rows, hd), 1) < 3 * heads
    neg = jnp.where(used, -1.0, 0.0).astype(BF)
    kloc[:, hd:] = neg
    vloc[:, hd:] = neg
    for j in range(2):
        js = slice(j * rows, (j + 1) * rows)
        kfar[js, hd:] = neg
        vfar[js, hd:] = neg
    for c in ins[6:]:
        c.wait()

    def near(g):
        head = row_h + g * grp
        hit = (row_l == head) | (row_l == head + heads) | (row_l == head + 2 * heads)
        keep = jnp.where(hit, 1.0, 0.0).astype(BF)
        sl = pl.ds(g * grp, grp)
        qa[g, :, :hd] = q_vm[:, sl, :].reshape(rows * grp, hd)
        da[g, :, :hd] = up_vm[:, sl, :].reshape(rows * grp, hd)
        qa[g, :, hd:] = (lse_l[:, None, :] * keep[None]).reshape(rows * grp, hd)
        da[g, :, hd:] = (del_l[:, None, :] * keep[None]).reshape(rows * grp, hd)
        kloc[:, :hd] = kv[g * 2][mine]
        vloc[:, :hd] = kv[g * 2 + 1][mine]
        x = lax.dot_general(qa[g], kloc[...], nt, preferred_element_type=F32)
        y = lax.dot_general(da[g], vloc[...], nt, preferred_element_type=F32)
        x = (x.reshape(rows, grp, rows) + bias[...][:, None, :]).reshape(rows * grp, rows)
        p = jnp.exp2(x * scale2)
        ds_low = (p * y).astype(BF)
        p_low = p.astype(BF)
        dq = jnp.dot(ds_low, kloc[:, :hd], preferred_element_type=F32)
        dk_loc[g] = lax.dot_general(ds_low, qa[g, :, :hd], tn, preferred_element_type=F32)
        dv_loc[g] = lax.dot_general(p_low, da[g, :, :hd], tn, preferred_element_type=F32)
        dq_vm[:, sl, :] = dq.reshape(rows, grp, hd)

    def listed(c, dst):
        for j in range(2):
            span = pairs_ref[j, me]
            dst[pl.ds(j * rows, rows), :hd] = kv[c][lax.rem(span, ss) * zs + lax.div(span, ss)]

    def peer_of(off):
        d = lax.rem(me + off, spans)
        return d, {"ctx": d // ss, "sub": lax.rem(d, ss)}

    def give(c, total):
        for j in range(2):
            part = total[j * rows:(j + 1) * rows].astype(BF)
            send_a[c * spans:(c + 1) * spans, j] = part.reshape(spans, stripe, hd)
        recv_a[c * spans + me] = send_a[c * spans + me]
        for off in range(1, spans):
            d, at = peer_of(off)
            pltpu.make_async_remote_copy(
                src_ref=send_a.at[c * spans + d], dst_ref=recv_a.at[c * spans + me],
                send_sem=a_send.at[0], recv_sem=a_recv.at[c],
                device_id=at, device_id_type=MESH).start()

    def far_keys(g):
        listed(g * 2, kfar)
        x = lax.dot_general(qa[g], kfar[...], nt, preferred_element_type=F32)
        p = jnp.exp2(x * scale2)
        probs[...] = p
        give(g * 2 + 1, lax.dot_general(p.astype(BF), da[g, :, :hd], tn, preferred_element_type=F32))

    def far_vals(g):
        listed(g * 2 + 1, vfar)
        y = lax.dot_general(da[g], vfar[...], nt, preferred_element_type=F32)
        ds_low = (probs[...] * y).astype(BF)
        give(g * 2, lax.dot_general(ds_low, qa[g, :, :hd], tn, preferred_element_type=F32))
        dq = jnp.dot(ds_low, kfar[:, :hd], preferred_element_type=F32).reshape(rows, grp, hd)
        sl = pl.ds(g * grp, grp)
        dq_vm[:, sl, :] = (dq_vm[:, sl, :] + dq) * factor

    def far(g):
        listed(g * 2, kfar)
        listed(g * 2 + 1, vfar)
        x = lax.dot_general(qa[g], kfar[...], nt, preferred_element_type=F32)
        y = lax.dot_general(da[g], vfar[...], nt, preferred_element_type=F32)
        p = jnp.exp2(x * scale2)
        ds_low = (p * y).astype(BF)
        dq = jnp.dot(ds_low, kfar[:, :hd], preferred_element_type=F32).reshape(rows, grp, hd)
        dk = lax.dot_general(ds_low, qa[g, :, :hd], tn, preferred_element_type=F32)
        dv = lax.dot_general(p.astype(BF), da[g, :, :hd], tn, preferred_element_type=F32)
        sl = pl.ds(g * grp, grp)
        dq_vm[:, sl, :] = (dq_vm[:, sl, :] + dq) * factor
        give(g * 2 + 1, dv)
        give(g * 2, dk)

    def many(ref, first, count, send_sem, recv_sem):
        return pltpu.make_async_remote_copy(
            src_ref=ref.at[pl.ds(first, count)], dst_ref=ref.at[pl.ds(first, count)],
            send_sem=send_sem, recv_sem=recv_sem,
            device_id={"ctx": z, "sub": other}, device_id_type=MESH)

    def combine(c):
        many(recv_a, c * spans, spans - 1, a_send.at[0], a_recv.at[c]).wait_recv()

        def owner(o, _):
            total = jnp.zeros((stripe, hd), F32)
            for src in range(spans):
                for j in range(2):
                    got = recv_a[c * spans + src, j].astype(F32)
                    total = total + jnp.where(pairs_ref[j, src] == o, got, 0.0)
            send_b[c * spans + o] = total.astype(BF)
            return 0

        lax.fori_loop(0, spans, owner, 0)
        recv_b[c * spans + me] = send_b[c * spans + me]
        for off in range(1, spans):
            d, at = peer_of(off)
            pltpu.make_async_remote_copy(
                src_ref=send_b.at[c * spans + d], dst_ref=recv_b.at[c * spans + me],
                send_sem=b_send.at[0], recv_sem=b_recv.at[c],
                device_id=at, device_id_type=MESH).start()

    def finish(c):
        g, part = c // 2, c % 2
        many(recv_b, c * spans, spans - 1, b_send.at[0], b_recv.at[c]).wait_recv()
        home = recv_b[c * spans:(c + 1) * spans].reshape(rows, hd).astype(F32)
        at = pl.ds(g, rows, stride=kvh)
        if part == 0:
            dk_ref[at, :] = (dk_loc[g] + home) * factor
        else:
            dv_ref[at, :] = dv_loc[g] + home

    def partner_wait(c):
        to_partner(c, pl.ds(other * zs, zs)).wait_recv()

    last = zs - 1
    for g in range(kvh):
        near(g)
        if g == 0:
            for c in range(2, chunks):
                own_step(c)
        relay_step(g * 2, 1)
        relay_step(g * 2 + 1, 1)
    for j in range(2, last):
        for c in range(chunks):
            relay_step(c, j)
    if last > 1:
        relay_step(0, last)
        relay_step(1, last)
    for g in range(kvh - 1):
        partner_wait(g * 2)
        partner_wait(g * 2 + 1)
        far(g)
        if last > 1:
            relay_step(g * 2 + 2, last)
            relay_step(g * 2 + 3, last)
    partner_wait(chunks - 2)
    far_keys(kvh - 1)
    partner_wait(chunks - 1)
    far_vals(kvh - 1)
    order = [g * 2 + part for g in range(kvh) for part in (1, 0)]
    for c in order:
        combine(c)
    for c in order:
        finish(c)
    for c in range(chunks):
        line_sent(c)
    many(send_a, 0, chunks * (spans - 1), a_send.at[0], a_recv.at[0]).wait_send()
    many(send_b, 0, chunks * (spans - 1), b_send.at[0], b_recv.at[0]).wait_send()


def tail_kernel(dq_vm, dk_vm, dv_vm, dq_out, dk_out, dv_out, sems):
    copies = [
        pltpu.make_async_copy(src, dst, sems.at[i])
        for i, (src, dst) in enumerate(((dq_vm, dq_out), (dk_vm, dk_out), (dv_vm, dv_out)))
    ]
    for c in copies:
        c.start()
    for c in copies:
        c.wait()


def written(dq, dk, dv):
    return pl.pallas_call(
        tail_kernel,
        out_shape=tuple(jax.ShapeDtypeStruct(x.shape, F32) for x in (dq, dk, dv)),
        in_specs=[pl.BlockSpec(memory_space=pltpu.VMEM)] * 3,
        out_specs=(pl.BlockSpec(memory_space=pltpu.HBM),) * 3,
        scratch_shapes=[pltpu.SemaphoreType.DMA((3,))],
        compiler_params=pltpu.CompilerParams(vmem_limit_bytes=4 * 1024 * 1024),
        name="write_out",
    )(dq, dk, dv)


def fused(zs, ss, queries, keys, values, grad_out, row_lse, row_delta, doc_ids, pairs):
    rows, qh, hd = queries.shape
    kvh = keys.shape[1]
    grp = qh // kvh
    spans = zs * ss
    stripe = rows // spans
    chunks = 2 * kvh
    vm = pl.BlockSpec(memory_space=pltpu.VMEM)
    hbm = pl.BlockSpec(memory_space=pltpu.HBM)
    dma = pltpu.SemaphoreType.DMA
    dq, dk, dv = pl.pallas_call(
        functools.partial(kernel, (zs, ss, rows, kvh, grp, hd)),
        out_shape=(
            pltpu.VMEM((rows, qh, hd), F32),
            pltpu.VMEM((rows * kvh, hd), F32),
            pltpu.VMEM((rows * kvh, hd), F32),
        ),
        in_specs=[hbm, hbm, hbm, hbm, hbm, hbm, hbm, hbm],
        out_specs=(vm, vm, vm),
        scratch_shapes=[
            pltpu.SMEM(pairs.shape[::-1], jnp.int32),
            pltpu.VMEM((1, rows), jnp.int32),
            pltpu.VMEM((qh, rows), F32),
            pltpu.VMEM((qh, rows), F32),
            pltpu.VMEM((rows * kvh, hd), BF),
            pltpu.VMEM((rows * kvh, hd), BF),
            pltpu.VMEM((rows, qh, hd), BF),
            pltpu.VMEM((rows, qh, hd), BF),
            pltpu.VMEM((kvh, rows * grp, 2 * hd), BF),
            pltpu.VMEM((kvh, rows * grp, 2 * hd), BF),
            pltpu.VMEM((rows, rows), F32),
            pltpu.VMEM((2 * rows, 2 * hd), BF),
            pltpu.VMEM((2 * rows, 2 * hd), BF),
            pltpu.VMEM((rows, 2 * hd), BF),
            pltpu.VMEM((rows, 2 * hd), BF),
            pltpu.VMEM((2, rows * kvh, hd), F32),
            pltpu.VMEM((rows * grp, 2 * rows), F32),
            pltpu.VMEM((kvh, rows, hd), F32),
            pltpu.VMEM((kvh, rows, hd), F32),
            [pltpu.VMEM((spans, rows, hd), BF) for _ in range(chunks)],
            pltpu.VMEM((chunks * spans, 2, stripe, hd), BF),
            pltpu.VMEM((chunks * spans, 2, stripe, hd), BF),
            pltpu.VMEM((chunks * spans, stripe, hd), BF),
            pltpu.VMEM((chunks * spans, stripe, hd), BF),
            dma((8,)),
            dma((chunks, 2)),
            dma((chunks,)),
            dma((chunks, zs)),
            dma((chunks,)),
            dma((1,)),
            dma((chunks,)),
            dma((1,)),
            dma((chunks,)),
        ],
        compiler_params=pltpu.CompilerParams(collective_id=0, has_side_effects=True),
        name="span_grads",
    )(
        pairs.T, doc_ids.reshape(1, rows), row_lse.T, row_delta.T,
        keys.reshape(rows * kvh, hd), values.reshape(rows * kvh, hd), queries, grad_out,
    )
    dq, dk, dv = written(dq, dk, dv)
    return dq, dk.reshape(rows, kvh, hd), dv.reshape(rows, kvh, hd)


QH = 64
KVH = 4


def block_terms(query_blk, upstream, log_norm, row_terms, key_blk, value_blk, allowed, factor):
    scores = (
        jnp.einsum("tghd,kgd->tghk", query_blk, key_blk, preferred_element_type=jnp.float32)
        * factor
    )
    probs = jnp.exp(scores - log_norm[..., None])
    if allowed is not None:
        probs = jnp.where(allowed[:, None, None, :], probs, 0.0)
    grad_probs = jnp.einsum(
        "tghd,kgd->tghk", upstream, value_blk, preferred_element_type=jnp.float32
    )
    grad_scores = probs * (grad_probs - row_terms[..., None])
    probs_low = probs.astype(jnp.bfloat16)
    scores_low = grad_scores.astype(jnp.bfloat16)
    grad_val = jnp.einsum("tghk,tghd->kgd", probs_low, upstream, preferred_element_type=jnp.float32)
    grad_key = (
        jnp.einsum("tghk,tghd->kgd", scores_low, query_blk, preferred_element_type=jnp.float32)
        * factor
    )
    grad_query = (
        jnp.einsum("tghk,kgd->tghd", scores_low, key_blk, preferred_element_type=jnp.float32)
        * factor
    )
    return (grad_query, grad_key, grad_val)


def body(zs, ss, queries, keys, values, grad_out, row_lse, row_delta, doc_ids, pairs):
    grp = queries.shape[1] // keys.shape[1]
    if (
        ss == 2
        and queries.shape[0] % (16 * zs * ss) == 0
        and grp % 16 == 0
        and 3 * queries.shape[1] <= queries.shape[2]
    ):
        return fused(
            zs, ss, queries, keys, values, grad_out, row_lse, row_delta, doc_ids, pairs
        )
    rows_here = queries.shape[0]
    heads_here = keys.shape[1]
    head_dim = keys.shape[2]
    grouped = QH // KVH
    factor = head_dim ** (-0.5)
    spans = lax.axis_size(("ctx", "sub"))
    stripe = rows_here // spans
    query_blk = queries.reshape(rows_here, heads_here, grouped, head_dim)
    upstream = grad_out.reshape(rows_here, heads_here, grouped, head_dim)
    log_norm = row_lse.reshape(rows_here, heads_here, grouped)
    row_terms = row_delta.reshape(rows_here, heads_here, grouped)
    positions = jnp.arange(rows_here, dtype=jnp.int32)
    allowed = (positions[:, None] >= positions[None, :]) & (doc_ids[:, None] == doc_ids[None, :])
    query_sum, key_local, value_local = block_terms(
        query_blk, upstream, log_norm, row_terms, keys, values, allowed, factor
    )
    stacked = jnp.concatenate([keys, values], axis=2).reshape(rows_here, heads_here * 2 * head_dim)
    features = stacked.shape[1]
    spread = lax.all_to_all(
        stacked.reshape(spans, stripe, features),
        ("ctx", "sub"),
        split_axis=0,
        concat_axis=0,
        tiled=True,
    )
    wanted = jnp.take(spread, pairs.T, axis=0)
    remote = lax.all_to_all(
        wanted, ("ctx", "sub"), split_axis=1, concat_axis=1, tiled=True
    ).reshape(2, rows_here, features)
    remote = remote.reshape(2, rows_here, heads_here, 2 * head_dim)
    returned = []
    for which in range(2):
        far_keys = remote[which, :, :, :head_dim]
        far_values = remote[which, :, :, head_dim:]
        query_part, key_part, value_part = block_terms(
            query_blk, upstream, log_norm, row_terms, far_keys, far_values, None, factor
        )
        query_sum = query_sum + query_part
        returned.append(
            jnp.concatenate([key_part, value_part], axis=2).reshape(rows_here, features)
        )
    outgoing = jnp.stack(returned).reshape(2, spans, stripe, features)
    incoming = lax.all_to_all(outgoing, ("ctx", "sub"), split_axis=1, concat_axis=1, tiled=True)
    owners = pairs.T.reshape(-1)
    select = (jnp.arange(spans, dtype=jnp.int32)[:, None] == owners[None, :]).astype(jnp.float32)
    summed = jnp.dot(
        select,
        incoming.reshape(2 * spans, stripe * features),
        precision=lax.Precision.HIGHEST,
        preferred_element_type=jnp.float32,
    )
    at_home = lax.all_to_all(
        summed.reshape(spans, stripe, features),
        ("ctx", "sub"),
        split_axis=0,
        concat_axis=0,
        tiled=True,
    )
    at_home = at_home.reshape(rows_here, heads_here, 2 * head_dim)
    grad_keys = key_local + at_home[:, :, :head_dim]
    grad_values = value_local + at_home[:, :, head_dim:]
    grad_queries = query_sum.reshape(rows_here, heads_here * grouped, head_dim)
    return (grad_queries, grad_keys, grad_values)


def solution(mesh):
    return jax.shard_map(
        functools.partial(body, mesh.shape["ctx"], mesh.shape["sub"]),
        mesh=mesh,
        in_specs=(
            P(("groups", "ctx", "sub"), "head", None),
            P(("groups", "ctx", "sub"), "head", None),
            P(("groups", "ctx", "sub"), "head", None),
            P(("groups", "ctx", "sub"), "head", None),
            P(("groups", "ctx", "sub"), "head"),
            P(("groups", "ctx", "sub"), "head"),
            P(("groups", "ctx", "sub")),
            P("groups", None),
        ),
        out_specs=(
            P(("groups", "ctx", "sub"), "head", None),
            P(("groups", "ctx", "sub"), "head", None),
            P(("groups", "ctx", "sub"), "head", None),
        ),
        check_vma=False,
    )
```

```python
import functools
import math

import jax
import jax.numpy as jnp
from jax import lax
from jax.experimental import pallas as pl
from jax.experimental.pallas import tpu as pltpu
from jax.sharding import PartitionSpec as P

BF = jnp.bfloat16
F32 = jnp.float32
MESH = pl.DeviceIdType.MESH


def pieces_of(x):
    hi = x.astype(BF)
    rest = x - hi.astype(F32)
    mid = rest.astype(BF)
    lo = (rest - mid.astype(F32)).astype(BF)
    return hi, mid, lo


def kernel(
    dims,
    pairs_hbm, docs_hbm, lse_hbm, delta_hbm, keys_hbm, vals_hbm, q_hbm, up_hbm,
    dq_vm, dk_ref, dv_ref,
    pairs_ref, docs_ref, lse_ref, delta_ref, keys_ref, vals_ref, q_vm, up_vm,
    qa, da, bias, kfar, vfar, kloc, vloc, wide, probs,
    dk_loc, dv_loc, kv, send_a, recv_a, send_b, recv_b,
    in_sem, z_send, p_send, z_recv, p_recv, a_send, a_recv, b_send, b_recv,
):
    zs, ss, rows, kvh, grp, hd = dims
    spans = zs * ss
    stripe = rows // spans
    chunks = 2 * kvh
    factor = hd ** -0.5
    scale2 = factor * math.log2(math.e)
    z = lax.axis_index("ctx")
    s = lax.axis_index("sub")
    me = z * ss + s
    other = 1 - s
    mine = s * zs + z
    nt = (((1,), (1,)), ((), ()))
    tn = (((0,), (0,)), ((), ()))

    barrier = pltpu.get_barrier_semaphore()

    def greet(dz, ds):
        pl.semaphore_signal(barrier, inc=1, device_id={"ctx": dz, "sub": ds}, device_id_type=MESH)

    greet(z, other)

    @pl.when(z > 0)
    def _():
        greet(z - 1, s)

    @pl.when(z < zs - 1)
    def _():
        greet(z + 1, s)

    ins = [
        pltpu.make_async_copy(src, dst, in_sem.at[i])
        for i, (src, dst) in enumerate((
            (keys_hbm, keys_ref), (vals_hbm, vals_ref), (lse_hbm, lse_ref), (delta_hbm, delta_ref),
            (docs_hbm, docs_ref), (pairs_hbm, pairs_ref), (q_hbm, q_vm), (up_hbm, up_vm),
        ))
    ]
    for c in ins[:6]:
        c.start()
    for part, ref in enumerate((keys_ref, vals_ref)):
        ins[part].wait()
        wide[part] = ref[...].astype(F32)
        for g in range(kvh):
            kv[g * 2 + part][mine] = wide[part, pl.ds(g, rows, stride=kvh), :].astype(BF)
    for c in ins[6:]:
        c.start()

    ends = jnp.where(z > 0, 1, 0) + jnp.where(z < zs - 1, 1, 0)
    pl.semaphore_wait(barrier, 1 + ends)

    def to_line(c, slot, from_z, dz, way):
        return pltpu.make_async_remote_copy(
            src_ref=kv[c].at[slot], dst_ref=kv[c].at[slot],
            send_sem=z_send.at[c, way], recv_sem=z_recv.at[c, from_z],
            device_id={"ctx": dz, "sub": s}, device_id_type=MESH)

    def to_partner(c, slots):
        return pltpu.make_async_remote_copy(
            src_ref=kv[c].at[slots], dst_ref=kv[c].at[slots],
            send_sem=p_send.at[c], recv_sem=p_recv.at[c],
            device_id={"ctx": z, "sub": other}, device_id_type=MESH)

    def own_step(c):
        @pl.when(z < zs - 1)
        def _():
            to_line(c, mine, z, z + 1, 0).start()

        @pl.when(z > 0)
        def _():
            to_line(c, mine, z, z - 1, 1).start()

        to_partner(c, mine).start()

    def relay_step(c, j):
        @pl.when(z >= j)
        def _():
            slot = mine - j
            to_line(c, slot, z - j, z, 0).wait_recv()

            @pl.when(z < zs - 1)
            def _():
                to_line(c, slot, z - j, z + 1, 0).start()

            to_partner(c, slot).start()

        @pl.when(z + j < zs)
        def _():
            slot = mine + j
            to_line(c, slot, z + j, z, 1).wait_recv()

            @pl.when(z > 0)
            def _():
                to_line(c, slot, z + j, z - 1, 1).start()

            to_partner(c, slot).start()

    def line_sent(c):
        for at in range(zs):
            @pl.when(z == at)
            def _():
                if at < zs - 1:
                    to_line(c, pl.ds(0, at + 1), at, z, 0).wait_send()
                if at > 0:
                    to_line(c, pl.ds(0, zs - at), at, z, 1).wait_send()

        to_partner(c, pl.ds(0, zs)).wait_send()

    for c in range(chunks):
        own_step(c)

    for c in ins[2:6]:
        c.wait()
    pos_t = lax.broadcasted_iota(jnp.int32, (rows, rows), 0)
    pos_u = lax.broadcasted_iota(jnp.int32, (rows, rows), 1)
    doc_u = jnp.broadcast_to(docs_ref[...].astype(F32), (rows, rows))
    doc_t = doc_u.T
    bias[...] = jnp.where((pos_t >= pos_u) & (doc_u == doc_t), 0.0, -3e38)

    heads = kvh * grp
    put_h = lax.broadcasted_iota(jnp.int32, (heads, hd), 0)
    put_l = lax.broadcasted_iota(jnp.int32, (heads, hd), 1)

    def lanes_of(x):
        total = jnp.zeros((rows, hd), F32)
        for i, piece in enumerate(pieces_of(x)):
            place = jnp.where(put_l == put_h + i * heads, 1.0, 0.0).astype(BF)
            total = total + lax.dot_general(piece, place, tn, preferred_element_type=F32)
        return total.astype(BF)

    lse_l = lanes_of(lse_ref[...] * (hd ** 0.5))
    del_l = lanes_of(delta_ref[...])
    row_h = lax.broadcasted_iota(jnp.int32, (grp, hd), 0)
    row_l = lax.broadcasted_iota(jnp.int32, (grp, hd), 1)
    used = lax.broadcasted_iota(jnp.int32, (rows, hd), 1) < 3 * heads
    neg = jnp.where(used, -1.0, 0.0).astype(BF)
    kloc[:, hd:] = neg
    vloc[:, hd:] = neg
    for j in range(2):
        js = slice(j * rows, (j + 1) * rows)
        kfar[js, hd:] = neg
        vfar[js, hd:] = neg
    for c in ins[6:]:
        c.wait()

    def near(g):
        head = row_h + g * grp
        hit = (row_l == head) | (row_l == head + heads) | (row_l == head + 2 * heads)
        keep = jnp.where(hit, 1.0, 0.0).astype(BF)
        sl = pl.ds(g * grp, grp)
        qa[g, :, :hd] = q_vm[:, sl, :].reshape(rows * grp, hd)
        da[g, :, :hd] = up_vm[:, sl, :].reshape(rows * grp, hd)
        qa[g, :, hd:] = (lse_l[:, None, :] * keep[None]).reshape(rows * grp, hd)
        da[g, :, hd:] = (del_l[:, None, :] * keep[None]).reshape(rows * grp, hd)
        kloc[:, :hd] = kv[g * 2][mine]
        vloc[:, :hd] = kv[g * 2 + 1][mine]
        x = lax.dot_general(qa[g], kloc[...], nt, preferred_element_type=F32)
        y = lax.dot_general(da[g], vloc[...], nt, preferred_element_type=F32)
        x = (x.reshape(rows, grp, rows) + bias[...][:, None, :]).reshape(rows * grp, rows)
        p = jnp.exp2(x * scale2)
        ds_low = (p * y).astype(BF)
        p_low = p.astype(BF)
        dq = jnp.dot(ds_low, kloc[:, :hd], preferred_element_type=F32)
        dk_loc[g] = lax.dot_general(ds_low, qa[g, :, :hd], tn, preferred_element_type=F32)
        dv_loc[g] = lax.dot_general(p_low, da[g, :, :hd], tn, preferred_element_type=F32)
        dq_vm[:, sl, :] = dq.reshape(rows, grp, hd)

    def listed(c, dst):
        for j in range(2):
            span = pairs_ref[j, me]
            dst[pl.ds(j * rows, rows), :hd] = kv[c][lax.rem(span, ss) * zs + lax.div(span, ss)]

    def peer_of(off):
        d = lax.rem(me + off, spans)
        return d, {"ctx": d // ss, "sub": lax.rem(d, ss)}

    def give(c, total):
        for j in range(2):
            part = total[j * rows:(j + 1) * rows].astype(BF)
            send_a[c * spans:(c + 1) * spans, j] = part.reshape(spans, stripe, hd)
        recv_a[c * spans + me] = send_a[c * spans + me]
        for off in range(1, spans):
            d, at = peer_of(off)
            pltpu.make_async_remote_copy(
                src_ref=send_a.at[c * spans + d], dst_ref=recv_a.at[c * spans + me],
                send_sem=a_send.at[0], recv_sem=a_recv.at[c],
                device_id=at, device_id_type=MESH).start()

    def far_keys(g):
        listed(g * 2, kfar)
        x = lax.dot_general(qa[g], kfar[...], nt, preferred_element_type=F32)
        p = jnp.exp2(x * scale2)
        probs[...] = p
        give(g * 2 + 1, lax.dot_general(p.astype(BF), da[g, :, :hd], tn, preferred_element_type=F32))

    def far_vals(g):
        listed(g * 2 + 1, vfar)
        y = lax.dot_general(da[g], vfar[...], nt, preferred_element_type=F32)
        ds_low = (probs[...] * y).astype(BF)
        give(g * 2, lax.dot_general(ds_low, qa[g, :, :hd], tn, preferred_element_type=F32))
        dq = jnp.dot(ds_low, kfar[:, :hd], preferred_element_type=F32).reshape(rows, grp, hd)
        sl = pl.ds(g * grp, grp)
        dq_vm[:, sl, :] = (dq_vm[:, sl, :] + dq) * factor

    def far(g):
        listed(g * 2, kfar)
        listed(g * 2 + 1, vfar)
        x = lax.dot_general(qa[g], kfar[...], nt, preferred_element_type=F32)
        y = lax.dot_general(da[g], vfar[...], nt, preferred_element_type=F32)
        p = jnp.exp2(x * scale2)
        ds_low = (p * y).astype(BF)
        dq = jnp.dot(ds_low, kfar[:, :hd], preferred_element_type=F32).reshape(rows, grp, hd)
        dk = lax.dot_general(ds_low, qa[g, :, :hd], tn, preferred_element_type=F32)
        dv = lax.dot_general(p.astype(BF), da[g, :, :hd], tn, preferred_element_type=F32)
        sl = pl.ds(g * grp, grp)
        dq_vm[:, sl, :] = (dq_vm[:, sl, :] + dq) * factor
        give(g * 2 + 1, dv)
        give(g * 2, dk)

    def many(ref, first, count, send_sem, recv_sem):
        return pltpu.make_async_remote_copy(
            src_ref=ref.at[pl.ds(first, count)], dst_ref=ref.at[pl.ds(first, count)],
            send_sem=send_sem, recv_sem=recv_sem,
            device_id={"ctx": z, "sub": other}, device_id_type=MESH)

    def combine(c):
        many(recv_a, c * spans, spans - 1, a_send.at[0], a_recv.at[c]).wait_recv()

        def owner(o, _):
            total = jnp.zeros((stripe, hd), F32)
            for src in range(spans):
                for j in range(2):
                    got = recv_a[c * spans + src, j].astype(F32)
                    total = total + jnp.where(pairs_ref[j, src] == o, got, 0.0)
            send_b[c * spans + o] = total.astype(BF)
            return 0

        lax.fori_loop(0, spans, owner, 0)
        recv_b[c * spans + me] = send_b[c * spans + me]
        for off in range(1, spans):
            d, at = peer_of(off)
            pltpu.make_async_remote_copy(
                src_ref=send_b.at[c * spans + d], dst_ref=recv_b.at[c * spans + me],
                send_sem=b_send.at[0], recv_sem=b_recv.at[c],
                device_id=at, device_id_type=MESH).start()

    def finish(c):
        g, part = c // 2, c % 2
        many(recv_b, c * spans, spans - 1, b_send.at[0], b_recv.at[c]).wait_recv()
        home = recv_b[c * spans:(c + 1) * spans].reshape(rows, hd).astype(F32)
        at = pl.ds(g, rows, stride=kvh)
        if part == 0:
            dk_ref[at, :] = (dk_loc[g] + home) * factor
        else:
            dv_ref[at, :] = dv_loc[g] + home

    def partner_wait(c):
        to_partner(c, pl.ds(other * zs, zs)).wait_recv()

    last = zs - 1
    for g in range(kvh):
        near(g)
        if g == 0:
            for c in range(chunks):
                relay_step(c, 1)
    for j in range(2, last):
        for c in range(chunks):
            relay_step(c, j)
    if last > 1:
        relay_step(0, last)
        relay_step(1, last)

    def next_two(g, core):
        @pl.when((s == core) & (last > 1))
        def _():
            relay_step(g * 2 + 2, last)
            relay_step(g * 2 + 3, last)

    for g in range(kvh - 1):
        next_two(g, ss - 1)
        partner_wait(g * 2)
        partner_wait(g * 2 + 1)
        far(g)
        next_two(g, 0)
    partner_wait(chunks - 2)
    far_keys(kvh - 1)
    partner_wait(chunks - 1)
    far_vals(kvh - 1)
    order = [g * 2 + part for g in range(kvh) for part in (1, 0)]
    for c in order:
        combine(c)
    for c in order:
        finish(c)
    for c in range(chunks):
        line_sent(c)
    many(send_a, 0, chunks * (spans - 1), a_send.at[0], a_recv.at[0]).wait_send()
    many(send_b, 0, chunks * (spans - 1), b_send.at[0], b_recv.at[0]).wait_send()


def tail_kernel(dq_vm, dk_vm, dv_vm, dq_out, dk_out, dv_out, sems):
    copies = [
        pltpu.make_async_copy(src, dst, sems.at[i])
        for i, (src, dst) in enumerate(((dq_vm, dq_out), (dk_vm, dk_out), (dv_vm, dv_out)))
    ]
    for c in copies:
        c.start()
    for c in copies:
        c.wait()


def written(dq, dk, dv):
    return pl.pallas_call(
        tail_kernel,
        out_shape=tuple(jax.ShapeDtypeStruct(x.shape, F32) for x in (dq, dk, dv)),
        in_specs=[pl.BlockSpec(memory_space=pltpu.VMEM)] * 3,
        out_specs=(pl.BlockSpec(memory_space=pltpu.HBM),) * 3,
        scratch_shapes=[pltpu.SemaphoreType.DMA((3,))],
        compiler_params=pltpu.CompilerParams(vmem_limit_bytes=4 * 1024 * 1024),
        name="write_out",
    )(dq, dk, dv)


def fused(zs, ss, queries, keys, values, grad_out, row_lse, row_delta, doc_ids, pairs):
    rows, qh, hd = queries.shape
    kvh = keys.shape[1]
    grp = qh // kvh
    spans = zs * ss
    stripe = rows // spans
    chunks = 2 * kvh
    vm = pl.BlockSpec(memory_space=pltpu.VMEM)
    hbm = pl.BlockSpec(memory_space=pltpu.HBM)
    dma = pltpu.SemaphoreType.DMA
    dq, dk, dv = pl.pallas_call(
        functools.partial(kernel, (zs, ss, rows, kvh, grp, hd)),
        out_shape=(
            pltpu.VMEM((rows, qh, hd), F32),
            pltpu.VMEM((rows * kvh, hd), F32),
            pltpu.VMEM((rows * kvh, hd), F32),
        ),
        in_specs=[hbm, hbm, hbm, hbm, hbm, hbm, hbm, hbm],
        out_specs=(vm, vm, vm),
        scratch_shapes=[
            pltpu.SMEM(pairs.shape[::-1], jnp.int32),
            pltpu.VMEM((1, rows), jnp.int32),
            pltpu.VMEM((qh, rows), F32),
            pltpu.VMEM((qh, rows), F32),
            pltpu.VMEM((rows * kvh, hd), BF),
            pltpu.VMEM((rows * kvh, hd), BF),
            pltpu.VMEM((rows, qh, hd), BF),
            pltpu.VMEM((rows, qh, hd), BF),
            pltpu.VMEM((kvh, rows * grp, 2 * hd), BF),
            pltpu.VMEM((kvh, rows * grp, 2 * hd), BF),
            pltpu.VMEM((rows, rows), F32),
            pltpu.VMEM((2 * rows, 2 * hd), BF),
            pltpu.VMEM((2 * rows, 2 * hd), BF),
            pltpu.VMEM((rows, 2 * hd), BF),
            pltpu.VMEM((rows, 2 * hd), BF),
            pltpu.VMEM((2, rows * kvh, hd), F32),
            pltpu.VMEM((rows * grp, 2 * rows), F32),
            pltpu.VMEM((kvh, rows, hd), F32),
            pltpu.VMEM((kvh, rows, hd), F32),
            [pltpu.VMEM((spans, rows, hd), BF) for _ in range(chunks)],
            pltpu.VMEM((chunks * spans, 2, stripe, hd), BF),
            pltpu.VMEM((chunks * spans, 2, stripe, hd), BF),
            pltpu.VMEM((chunks * spans, stripe, hd), BF),
            pltpu.VMEM((chunks * spans, stripe, hd), BF),
            dma((8,)),
            dma((chunks, 2)),
            dma((chunks,)),
            dma((chunks, zs)),
            dma((chunks,)),
            dma((1,)),
            dma((chunks,)),
            dma((1,)),
            dma((chunks,)),
        ],
        compiler_params=pltpu.CompilerParams(collective_id=0, has_side_effects=True),
        name="span_grads",
    )(
        pairs.T, doc_ids.reshape(1, rows), row_lse.T, row_delta.T,
        keys.reshape(rows * kvh, hd), values.reshape(rows * kvh, hd), queries, grad_out,
    )
    dq, dk, dv = written(dq, dk, dv)
    return dq, dk.reshape(rows, kvh, hd), dv.reshape(rows, kvh, hd)


QH = 64
KVH = 4


def block_terms(query_blk, upstream, log_norm, row_terms, key_blk, value_blk, allowed, factor):
    scores = (
        jnp.einsum("tghd,kgd->tghk", query_blk, key_blk, preferred_element_type=jnp.float32)
        * factor
    )
    probs = jnp.exp(scores - log_norm[..., None])
    if allowed is not None:
        probs = jnp.where(allowed[:, None, None, :], probs, 0.0)
    grad_probs = jnp.einsum(
        "tghd,kgd->tghk", upstream, value_blk, preferred_element_type=jnp.float32
    )
    grad_scores = probs * (grad_probs - row_terms[..., None])
    probs_low = probs.astype(jnp.bfloat16)
    scores_low = grad_scores.astype(jnp.bfloat16)
    grad_val = jnp.einsum("tghk,tghd->kgd", probs_low, upstream, preferred_element_type=jnp.float32)
    grad_key = (
        jnp.einsum("tghk,tghd->kgd", scores_low, query_blk, preferred_element_type=jnp.float32)
        * factor
    )
    grad_query = (
        jnp.einsum("tghk,kgd->tghd", scores_low, key_blk, preferred_element_type=jnp.float32)
        * factor
    )
    return (grad_query, grad_key, grad_val)


def body(zs, ss, queries, keys, values, grad_out, row_lse, row_delta, doc_ids, pairs):
    grp = queries.shape[1] // keys.shape[1]
    if (
        ss == 2
        and queries.shape[0] % (16 * zs * ss) == 0
        and grp % 16 == 0
        and 3 * queries.shape[1] <= queries.shape[2]
    ):
        return fused(
            zs, ss, queries, keys, values, grad_out, row_lse, row_delta, doc_ids, pairs
        )
    rows_here = queries.shape[0]
    heads_here = keys.shape[1]
    head_dim = keys.shape[2]
    grouped = QH // KVH
    factor = head_dim ** (-0.5)
    spans = lax.axis_size(("ctx", "sub"))
    stripe = rows_here // spans
    query_blk = queries.reshape(rows_here, heads_here, grouped, head_dim)
    upstream = grad_out.reshape(rows_here, heads_here, grouped, head_dim)
    log_norm = row_lse.reshape(rows_here, heads_here, grouped)
    row_terms = row_delta.reshape(rows_here, heads_here, grouped)
    positions = jnp.arange(rows_here, dtype=jnp.int32)
    allowed = (positions[:, None] >= positions[None, :]) & (doc_ids[:, None] == doc_ids[None, :])
    query_sum, key_local, value_local = block_terms(
        query_blk, upstream, log_norm, row_terms, keys, values, allowed, factor
    )
    stacked = jnp.concatenate([keys, values], axis=2).reshape(rows_here, heads_here * 2 * head_dim)
    features = stacked.shape[1]
    spread = lax.all_to_all(
        stacked.reshape(spans, stripe, features),
        ("ctx", "sub"),
        split_axis=0,
        concat_axis=0,
        tiled=True,
    )
    wanted = jnp.take(spread, pairs.T, axis=0)
    remote = lax.all_to_all(
        wanted, ("ctx", "sub"), split_axis=1, concat_axis=1, tiled=True
    ).reshape(2, rows_here, features)
    remote = remote.reshape(2, rows_here, heads_here, 2 * head_dim)
    returned = []
    for which in range(2):
        far_keys = remote[which, :, :, :head_dim]
        far_values = remote[which, :, :, head_dim:]
        query_part, key_part, value_part = block_terms(
            query_blk, upstream, log_norm, row_terms, far_keys, far_values, None, factor
        )
        query_sum = query_sum + query_part
        returned.append(
            jnp.concatenate([key_part, value_part], axis=2).reshape(rows_here, features)
        )
    outgoing = jnp.stack(returned).reshape(2, spans, stripe, features)
    incoming = lax.all_to_all(outgoing, ("ctx", "sub"), split_axis=1, concat_axis=1, tiled=True)
    owners = pairs.T.reshape(-1)
    select = (jnp.arange(spans, dtype=jnp.int32)[:, None] == owners[None, :]).astype(jnp.float32)
    summed = jnp.dot(
        select,
        incoming.reshape(2 * spans, stripe * features),
        precision=lax.Precision.HIGHEST,
        preferred_element_type=jnp.float32,
    )
    at_home = lax.all_to_all(
        summed.reshape(spans, stripe, features),
        ("ctx", "sub"),
        split_axis=0,
        concat_axis=0,
        tiled=True,
    )
    at_home = at_home.reshape(rows_here, heads_here, 2 * head_dim)
    grad_keys = key_local + at_home[:, :, :head_dim]
    grad_values = value_local + at_home[:, :, head_dim:]
    grad_queries = query_sum.reshape(rows_here, heads_here * grouped, head_dim)
    return (grad_queries, grad_keys, grad_values)


def solution(mesh):
    return jax.shard_map(
        functools.partial(body, mesh.shape["ctx"], mesh.shape["sub"]),
        mesh=mesh,
        in_specs=(
            P(("groups", "ctx", "sub"), "head", None),
            P(("groups", "ctx", "sub"), "head", None),
            P(("groups", "ctx", "sub"), "head", None),
            P(("groups", "ctx", "sub"), "head", None),
            P(("groups", "ctx", "sub"), "head"),
            P(("groups", "ctx", "sub"), "head"),
            P(("groups", "ctx", "sub")),
            P("groups", None),
        ),
        out_specs=(
            P(("groups", "ctx", "sub"), "head", None),
            P(("groups", "ctx", "sub"), "head", None),
            P(("groups", "ctx", "sub"), "head", None),
        ),
        check_vma=False,
    )
```

```python
import functools
import math

import jax
import jax.numpy as jnp
from jax import lax
from jax.experimental import pallas as pl
from jax.experimental.pallas import tpu as pltpu
from jax.sharding import PartitionSpec as P

BF = jnp.bfloat16
F32 = jnp.float32
MESH = pl.DeviceIdType.MESH


def pieces_of(x):
    hi = x.astype(BF)
    rest = x - hi.astype(F32)
    mid = rest.astype(BF)
    lo = (rest - mid.astype(F32)).astype(BF)
    return hi, mid, lo


def kernel(
    dims,
    pairs_hbm, docs_hbm, lse_hbm, delta_hbm, keys_hbm, vals_hbm, q_hbm, up_hbm,
    dq_vm, dk_ref, dv_ref,
    pairs_ref, docs_ref, lse_ref, delta_ref, keys_ref, vals_ref, q_vm, up_vm,
    qa, da, bias, kfar, vfar, kloc, vloc, wide, probs,
    dk_loc, dv_loc, kv, send_a, recv_a, send_b, recv_b,
    in_sem, z_send, p_send, z_recv, p_recv, a_send, a_recv, b_send, b_recv,
):
    zs, ss, rows, kvh, grp, hd = dims
    spans = zs * ss
    stripe = rows // spans
    chunks = 2 * kvh
    factor = hd ** -0.5
    scale2 = factor * math.log2(math.e)
    z = lax.axis_index("ctx")
    s = lax.axis_index("sub")
    me = z * ss + s
    other = 1 - s
    mine = s * zs + z
    nt = (((1,), (1,)), ((), ()))
    tn = (((0,), (0,)), ((), ()))
    skip = zs > 3

    barrier = pltpu.get_barrier_semaphore()

    def greet(dz, ds):
        pl.semaphore_signal(barrier, inc=1, device_id={"ctx": dz, "sub": ds}, device_id_type=MESH)

    greet(z, other)

    @pl.when(z > 0)
    def _():
        greet(z - 1, s)

    @pl.when(z < zs - 1)
    def _():
        greet(z + 1, s)

    if skip:
        @pl.when(z == 2)
        def _():
            greet(0, s)

        @pl.when(z == zs - 3)
        def _():
            greet(zs - 1, s)

    ins = [
        pltpu.make_async_copy(src, dst, in_sem.at[i])
        for i, (src, dst) in enumerate((
            (keys_hbm, keys_ref), (vals_hbm, vals_ref), (lse_hbm, lse_ref), (delta_hbm, delta_ref),
            (docs_hbm, docs_ref), (pairs_hbm, pairs_ref), (q_hbm, q_vm), (up_hbm, up_vm),
        ))
    ]
    for c in ins[:6]:
        c.start()
    for part, ref in enumerate((keys_ref, vals_ref)):
        ins[part].wait()
        wide[part] = ref[...].astype(F32)
        for g in range(kvh):
            kv[g * 2 + part][mine] = wide[part, pl.ds(g, rows, stride=kvh), :].astype(BF)
    for c in ins[6:]:
        c.start()

    ends = jnp.where(z > 0, 1, 0) + jnp.where(z < zs - 1, 1, 0)
    if skip:
        ends = ends + jnp.where((z == 0) | (z == zs - 1), 1, 0)
    pl.semaphore_wait(barrier, 1 + ends)

    def to_line(c, slot, from_z, dz, way):
        return pltpu.make_async_remote_copy(
            src_ref=kv[c].at[slot], dst_ref=kv[c].at[slot],
            send_sem=z_send.at[c, way], recv_sem=z_recv.at[c, from_z],
            device_id={"ctx": dz, "sub": s}, device_id_type=MESH)

    def to_partner(c, slots):
        return pltpu.make_async_remote_copy(
            src_ref=kv[c].at[slots], dst_ref=kv[c].at[slots],
            send_sem=p_send.at[c], recv_sem=p_recv.at[c],
            device_id={"ctx": z, "sub": other}, device_id_type=MESH)

    def own_step(c):
        if skip:
            @pl.when(z == 0)
            def _():
                to_line(c, mine, z, 2, 0).start()

            @pl.when(z == zs - 1)
            def _():
                to_line(c, mine, z, zs - 3, 1).start()

        @pl.when(z < zs - 1)
        def _():
            to_line(c, mine, z, z + 1, 0).start()

        @pl.when(z > 0)
        def _():
            to_line(c, mine, z, z - 1, 1).start()

        to_partner(c, mine).start()

    def relay_step(c, j):
        @pl.when(z >= j)
        def _():
            slot = mine - j
            to_line(c, slot, z - j, z, 0).wait_recv()

            @pl.when((z < zs - 1) & ((z > 1) | (not skip)))
            def _():
                to_line(c, slot, z - j, z + 1, 0).start()

            to_partner(c, slot).start()

        @pl.when(z + j < zs)
        def _():
            slot = mine + j
            to_line(c, slot, z + j, z, 1).wait_recv()

            @pl.when((z > 0) & ((z < zs - 2) | (not skip)))
            def _():
                to_line(c, slot, z + j, z - 1, 1).start()

            to_partner(c, slot).start()

    def line_sent(c):
        for at in range(zs):
            @pl.when(z == at)
            def _():
                for way, behind in enumerate((at, zs - 1 - at)):
                    count = behind + 1
                    if skip:
                        count += (behind == 0) - (behind == 1)
                    if behind < zs - 1:
                        to_line(c, pl.ds(0, count), at, z, way).wait_send()

        to_partner(c, pl.ds(0, zs)).wait_send()

    for c in range(chunks):
        own_step(c)

    for c in ins[2:6]:
        c.wait()
    pos_t = lax.broadcasted_iota(jnp.int32, (rows, rows), 0)
    pos_u = lax.broadcasted_iota(jnp.int32, (rows, rows), 1)
    doc_u = jnp.broadcast_to(docs_ref[...].astype(F32), (rows, rows))
    doc_t = doc_u.T
    bias[...] = jnp.where((pos_t >= pos_u) & (doc_u == doc_t), 0.0, -3e38)

    heads = kvh * grp
    put_h = lax.broadcasted_iota(jnp.int32, (heads, hd), 0)
    put_l = lax.broadcasted_iota(jnp.int32, (heads, hd), 1)

    def lanes_of(x):
        total = jnp.zeros((rows, hd), F32)
        for i, piece in enumerate(pieces_of(x)):
            place = jnp.where(put_l == put_h + i * heads, 1.0, 0.0).astype(BF)
            total = total + lax.dot_general(piece, place, tn, preferred_element_type=F32)
        return total.astype(BF)

    lse_l = lanes_of(lse_ref[...] * (hd ** 0.5))
    del_l = lanes_of(delta_ref[...])
    row_h = lax.broadcasted_iota(jnp.int32, (grp, hd), 0)
    row_l = lax.broadcasted_iota(jnp.int32, (grp, hd), 1)
    used = lax.broadcasted_iota(jnp.int32, (rows, hd), 1) < 3 * heads
    neg = jnp.where(used, -1.0, 0.0).astype(BF)
    kloc[:, hd:] = neg
    vloc[:, hd:] = neg
    for j in range(2):
        js = slice(j * rows, (j + 1) * rows)
        kfar[js, hd:] = neg
        vfar[js, hd:] = neg
    for c in ins[6:]:
        c.wait()

    def near(g):
        head = row_h + g * grp
        hit = (row_l == head) | (row_l == head + heads) | (row_l == head + 2 * heads)
        keep = jnp.where(hit, 1.0, 0.0).astype(BF)
        sl = pl.ds(g * grp, grp)
        qa[g, :, :hd] = q_vm[:, sl, :].reshape(rows * grp, hd)
        da[g, :, :hd] = up_vm[:, sl, :].reshape(rows * grp, hd)
        qa[g, :, hd:] = (lse_l[:, None, :] * keep[None]).reshape(rows * grp, hd)
        da[g, :, hd:] = (del_l[:, None, :] * keep[None]).reshape(rows * grp, hd)
        kloc[:, :hd] = kv[g * 2][mine]
        vloc[:, :hd] = kv[g * 2 + 1][mine]
        x = lax.dot_general(qa[g], kloc[...], nt, preferred_element_type=F32)
        y = lax.dot_general(da[g], vloc[...], nt, preferred_element_type=F32)
        x = (x.reshape(rows, grp, rows) + bias[...][:, None, :]).reshape(rows * grp, rows)
        p = jnp.exp2(x * scale2)
        ds_low = (p * y).astype(BF)
        p_low = p.astype(BF)
        dq = jnp.dot(ds_low, kloc[:, :hd], preferred_element_type=F32)
        dk_loc[g] = lax.dot_general(ds_low, qa[g, :, :hd], tn, preferred_element_type=F32)
        dv_loc[g] = lax.dot_general(p_low, da[g, :, :hd], tn, preferred_element_type=F32)
        dq_vm[:, sl, :] = dq.reshape(rows, grp, hd)

    def listed(c, dst):
        for j in range(2):
            span = pairs_ref[j, me]
            dst[pl.ds(j * rows, rows), :hd] = kv[c][lax.rem(span, ss) * zs + lax.div(span, ss)]

    def peer_of(off):
        d = lax.rem(me + off, spans)
        return d, {"ctx": d // ss, "sub": lax.rem(d, ss)}

    def give(c, total):
        for j in range(2):
            part = total[j * rows:(j + 1) * rows].astype(BF)
            send_a[c * spans:(c + 1) * spans, j] = part.reshape(spans, stripe, hd)
        recv_a[c * spans + me] = send_a[c * spans + me]
        for off in range(1, spans):
            d, at = peer_of(off)
            pltpu.make_async_remote_copy(
                src_ref=send_a.at[c * spans + d], dst_ref=recv_a.at[c * spans + me],
                send_sem=a_send.at[0], recv_sem=a_recv.at[c],
                device_id=at, device_id_type=MESH).start()

    def far_keys(g):
        listed(g * 2, kfar)
        x = lax.dot_general(qa[g], kfar[...], nt, preferred_element_type=F32)
        p = jnp.exp2(x * scale2)
        probs[...] = p
        give(g * 2 + 1, lax.dot_general(p.astype(BF), da[g, :, :hd], tn, preferred_element_type=F32))

    def far_vals(g):
        listed(g * 2 + 1, vfar)
        y = lax.dot_general(da[g], vfar[...], nt, preferred_element_type=F32)
        ds_low = (probs[...] * y).astype(BF)
        give(g * 2, lax.dot_general(ds_low, qa[g, :, :hd], tn, preferred_element_type=F32))
        dq = jnp.dot(ds_low, kfar[:, :hd], preferred_element_type=F32).reshape(rows, grp, hd)
        sl = pl.ds(g * grp, grp)
        dq_vm[:, sl, :] = (dq_vm[:, sl, :] + dq) * factor

    def far(g):
        listed(g * 2, kfar)
        listed(g * 2 + 1, vfar)
        x = lax.dot_general(qa[g], kfar[...], nt, preferred_element_type=F32)
        y = lax.dot_general(da[g], vfar[...], nt, preferred_element_type=F32)
        p = jnp.exp2(x * scale2)
        ds_low = (p * y).astype(BF)
        dq = jnp.dot(ds_low, kfar[:, :hd], preferred_element_type=F32).reshape(rows, grp, hd)
        dk = lax.dot_general(ds_low, qa[g, :, :hd], tn, preferred_element_type=F32)
        dv = lax.dot_general(p.astype(BF), da[g, :, :hd], tn, preferred_element_type=F32)
        sl = pl.ds(g * grp, grp)
        dq_vm[:, sl, :] = (dq_vm[:, sl, :] + dq) * factor
        give(g * 2 + 1, dv)
        give(g * 2, dk)

    def many(ref, first, count, send_sem, recv_sem):
        return pltpu.make_async_remote_copy(
            src_ref=ref.at[pl.ds(first, count)], dst_ref=ref.at[pl.ds(first, count)],
            send_sem=send_sem, recv_sem=recv_sem,
            device_id={"ctx": z, "sub": other}, device_id_type=MESH)

    def combine(c):
        many(recv_a, c * spans, spans - 1, a_send.at[0], a_recv.at[c]).wait_recv()

        def owner(o, _):
            total = jnp.zeros((stripe, hd), F32)
            for src in range(spans):
                for j in range(2):
                    got = recv_a[c * spans + src, j].astype(F32)
                    total = total + jnp.where(pairs_ref[j, src] == o, got, 0.0)
            send_b[c * spans + o] = total.astype(BF)
            return 0

        lax.fori_loop(0, spans, owner, 0)
        recv_b[c * spans + me] = send_b[c * spans + me]
        for off in range(1, spans):
            d, at = peer_of(off)
            pltpu.make_async_remote_copy(
                src_ref=send_b.at[c * spans + d], dst_ref=recv_b.at[c * spans + me],
                send_sem=b_send.at[0], recv_sem=b_recv.at[c],
                device_id=at, device_id_type=MESH).start()

    def finish(c):
        g, part = c // 2, c % 2
        many(recv_b, c * spans, spans - 1, b_send.at[0], b_recv.at[c]).wait_recv()
        home = recv_b[c * spans:(c + 1) * spans].reshape(rows, hd).astype(F32)
        at = pl.ds(g, rows, stride=kvh)
        if part == 0:
            dk_ref[at, :] = (dk_loc[g] + home) * factor
        else:
            dv_ref[at, :] = dv_loc[g] + home

    def partner_wait(c):
        to_partner(c, pl.ds(other * zs, zs)).wait_recv()

    last = zs - 1
    middle = (z > 0) & (z < last)

    def second(where):
        @pl.when(where & (last > 2))
        def _():
            relay_step(0, 2)
            relay_step(1, 2)

    for g in range(kvh):
        near(g)
        if g == 0:
            for c in range(chunks):
                relay_step(c, 1)
            second(middle)
    second(jnp.logical_not(middle))
    for j in range(2, last):
        for c in range(2 if j == 2 else 0, chunks):
            relay_step(c, j)
    if last > 1:
        relay_step(0, last)
        relay_step(1, last)

    def next_two(g, core):
        @pl.when((s == core) & (last > 1))
        def _():
            relay_step(g * 2 + 2, last)
            relay_step(g * 2 + 3, last)

    for g in range(kvh - 1):
        next_two(g, ss - 1)
        partner_wait(g * 2)
        partner_wait(g * 2 + 1)
        far(g)
        next_two(g, 0)
    partner_wait(chunks - 2)
    far_keys(kvh - 1)
    partner_wait(chunks - 1)
    far_vals(kvh - 1)
    order = [g * 2 + part for g in range(kvh) for part in (1, 0)]
    for c in order:
        combine(c)
    for c in order:
        finish(c)
    for c in range(chunks):
        line_sent(c)
    many(send_a, 0, chunks * (spans - 1), a_send.at[0], a_recv.at[0]).wait_send()
    many(send_b, 0, chunks * (spans - 1), b_send.at[0], b_recv.at[0]).wait_send()


def tail_kernel(dq_vm, dk_vm, dv_vm, dq_out, dk_out, dv_out, sems):
    copies = [
        pltpu.make_async_copy(src, dst, sems.at[i])
        for i, (src, dst) in enumerate(((dq_vm, dq_out), (dk_vm, dk_out), (dv_vm, dv_out)))
    ]
    for c in copies:
        c.start()
    for c in copies:
        c.wait()


def written(dq, dk, dv):
    return pl.pallas_call(
        tail_kernel,
        out_shape=tuple(jax.ShapeDtypeStruct(x.shape, F32) for x in (dq, dk, dv)),
        in_specs=[pl.BlockSpec(memory_space=pltpu.VMEM)] * 3,
        out_specs=(pl.BlockSpec(memory_space=pltpu.HBM),) * 3,
        scratch_shapes=[pltpu.SemaphoreType.DMA((3,))],
        compiler_params=pltpu.CompilerParams(vmem_limit_bytes=4 * 1024 * 1024),
        name="write_out",
    )(dq, dk, dv)


def fused(zs, ss, queries, keys, values, grad_out, row_lse, row_delta, doc_ids, pairs):
    rows, qh, hd = queries.shape
    kvh = keys.shape[1]
    grp = qh // kvh
    spans = zs * ss
    stripe = rows // spans
    chunks = 2 * kvh
    vm = pl.BlockSpec(memory_space=pltpu.VMEM)
    hbm = pl.BlockSpec(memory_space=pltpu.HBM)
    dma = pltpu.SemaphoreType.DMA
    dq, dk, dv = pl.pallas_call(
        functools.partial(kernel, (zs, ss, rows, kvh, grp, hd)),
        out_shape=(
            pltpu.VMEM((rows, qh, hd), F32),
            pltpu.VMEM((rows * kvh, hd), F32),
            pltpu.VMEM((rows * kvh, hd), F32),
        ),
        in_specs=[hbm, hbm, hbm, hbm, hbm, hbm, hbm, hbm],
        out_specs=(vm, vm, vm),
        scratch_shapes=[
            pltpu.SMEM(pairs.shape[::-1], jnp.int32),
            pltpu.VMEM((1, rows), jnp.int32),
            pltpu.VMEM((qh, rows), F32),
            pltpu.VMEM((qh, rows), F32),
            pltpu.VMEM((rows * kvh, hd), BF),
            pltpu.VMEM((rows * kvh, hd), BF),
            pltpu.VMEM((rows, qh, hd), BF),
            pltpu.VMEM((rows, qh, hd), BF),
            pltpu.VMEM((kvh, rows * grp, 2 * hd), BF),
            pltpu.VMEM((kvh, rows * grp, 2 * hd), BF),
            pltpu.VMEM((rows, rows), F32),
            pltpu.VMEM((2 * rows, 2 * hd), BF),
            pltpu.VMEM((2 * rows, 2 * hd), BF),
            pltpu.VMEM((rows, 2 * hd), BF),
            pltpu.VMEM((rows, 2 * hd), BF),
            pltpu.VMEM((2, rows * kvh, hd), F32),
            pltpu.VMEM((rows * grp, 2 * rows), F32),
            pltpu.VMEM((kvh, rows, hd), F32),
            pltpu.VMEM((kvh, rows, hd), F32),
            [pltpu.VMEM((spans, rows, hd), BF) for _ in range(chunks)],
            pltpu.VMEM((chunks * spans, 2, stripe, hd), BF),
            pltpu.VMEM((chunks * spans, 2, stripe, hd), BF),
            pltpu.VMEM((chunks * spans, stripe, hd), BF),
            pltpu.VMEM((chunks * spans, stripe, hd), BF),
            dma((8,)),
            dma((chunks, 2)),
            dma((chunks,)),
            dma((chunks, zs)),
            dma((chunks,)),
            dma((1,)),
            dma((chunks,)),
            dma((1,)),
            dma((chunks,)),
        ],
        compiler_params=pltpu.CompilerParams(collective_id=0, has_side_effects=True),
        name="span_grads",
    )(
        pairs.T, doc_ids.reshape(1, rows), row_lse.T, row_delta.T,
        keys.reshape(rows * kvh, hd), values.reshape(rows * kvh, hd), queries, grad_out,
    )
    dq, dk, dv = written(dq, dk, dv)
    return dq, dk.reshape(rows, kvh, hd), dv.reshape(rows, kvh, hd)


QH = 64
KVH = 4


def block_terms(query_blk, upstream, log_norm, row_terms, key_blk, value_blk, allowed, factor):
    scores = (
        jnp.einsum("tghd,kgd->tghk", query_blk, key_blk, preferred_element_type=jnp.float32)
        * factor
    )
    probs = jnp.exp(scores - log_norm[..., None])
    if allowed is not None:
        probs = jnp.where(allowed[:, None, None, :], probs, 0.0)
    grad_probs = jnp.einsum(
        "tghd,kgd->tghk", upstream, value_blk, preferred_element_type=jnp.float32
    )
    grad_scores = probs * (grad_probs - row_terms[..., None])
    probs_low = probs.astype(jnp.bfloat16)
    scores_low = grad_scores.astype(jnp.bfloat16)
    grad_val = jnp.einsum("tghk,tghd->kgd", probs_low, upstream, preferred_element_type=jnp.float32)
    grad_key = (
        jnp.einsum("tghk,tghd->kgd", scores_low, query_blk, preferred_element_type=jnp.float32)
        * factor
    )
    grad_query = (
        jnp.einsum("tghk,kgd->tghd", scores_low, key_blk, preferred_element_type=jnp.float32)
        * factor
    )
    return (grad_query, grad_key, grad_val)


def body(zs, ss, queries, keys, values, grad_out, row_lse, row_delta, doc_ids, pairs):
    grp = queries.shape[1] // keys.shape[1]
    if (
        ss == 2
        and queries.shape[0] % (16 * zs * ss) == 0
        and grp % 16 == 0
        and 3 * queries.shape[1] <= queries.shape[2]
    ):
        return fused(
            zs, ss, queries, keys, values, grad_out, row_lse, row_delta, doc_ids, pairs
        )
    rows_here = queries.shape[0]
    heads_here = keys.shape[1]
    head_dim = keys.shape[2]
    grouped = QH // KVH
    factor = head_dim ** (-0.5)
    spans = lax.axis_size(("ctx", "sub"))
    stripe = rows_here // spans
    query_blk = queries.reshape(rows_here, heads_here, grouped, head_dim)
    upstream = grad_out.reshape(rows_here, heads_here, grouped, head_dim)
    log_norm = row_lse.reshape(rows_here, heads_here, grouped)
    row_terms = row_delta.reshape(rows_here, heads_here, grouped)
    positions = jnp.arange(rows_here, dtype=jnp.int32)
    allowed = (positions[:, None] >= positions[None, :]) & (doc_ids[:, None] == doc_ids[None, :])
    query_sum, key_local, value_local = block_terms(
        query_blk, upstream, log_norm, row_terms, keys, values, allowed, factor
    )
    stacked = jnp.concatenate([keys, values], axis=2).reshape(rows_here, heads_here * 2 * head_dim)
    features = stacked.shape[1]
    spread = lax.all_to_all(
        stacked.reshape(spans, stripe, features),
        ("ctx", "sub"),
        split_axis=0,
        concat_axis=0,
        tiled=True,
    )
    wanted = jnp.take(spread, pairs.T, axis=0)
    remote = lax.all_to_all(
        wanted, ("ctx", "sub"), split_axis=1, concat_axis=1, tiled=True
    ).reshape(2, rows_here, features)
    remote = remote.reshape(2, rows_here, heads_here, 2 * head_dim)
    returned = []
    for which in range(2):
        far_keys = remote[which, :, :, :head_dim]
        far_values = remote[which, :, :, head_dim:]
        query_part, key_part, value_part = block_terms(
            query_blk, upstream, log_norm, row_terms, far_keys, far_values, None, factor
        )
        query_sum = query_sum + query_part
        returned.append(
            jnp.concatenate([key_part, value_part], axis=2).reshape(rows_here, features)
        )
    outgoing = jnp.stack(returned).reshape(2, spans, stripe, features)
    incoming = lax.all_to_all(outgoing, ("ctx", "sub"), split_axis=1, concat_axis=1, tiled=True)
    owners = pairs.T.reshape(-1)
    select = (jnp.arange(spans, dtype=jnp.int32)[:, None] == owners[None, :]).astype(jnp.float32)
    summed = jnp.dot(
        select,
        incoming.reshape(2 * spans, stripe * features),
        precision=lax.Precision.HIGHEST,
        preferred_element_type=jnp.float32,
    )
    at_home = lax.all_to_all(
        summed.reshape(spans, stripe, features),
        ("ctx", "sub"),
        split_axis=0,
        concat_axis=0,
        tiled=True,
    )
    at_home = at_home.reshape(rows_here, heads_here, 2 * head_dim)
    grad_keys = key_local + at_home[:, :, :head_dim]
    grad_values = value_local + at_home[:, :, head_dim:]
    grad_queries = query_sum.reshape(rows_here, heads_here * grouped, head_dim)
    return (grad_queries, grad_keys, grad_values)


def solution(mesh):
    return jax.shard_map(
        functools.partial(body, mesh.shape["ctx"], mesh.shape["sub"]),
        mesh=mesh,
        in_specs=(
            P(("groups", "ctx", "sub"), "head", None),
            P(("groups", "ctx", "sub"), "head", None),
            P(("groups", "ctx", "sub"), "head", None),
            P(("groups", "ctx", "sub"), "head", None),
            P(("groups", "ctx", "sub"), "head"),
            P(("groups", "ctx", "sub"), "head"),
            P(("groups", "ctx", "sub")),
            P("groups", None),
        ),
        out_specs=(
            P(("groups", "ctx", "sub"), "head", None),
            P(("groups", "ctx", "sub"), "head", None),
            P(("groups", "ctx", "sub"), "head", None),
        ),
        check_vma=False,
    )
```
